128 devices in a mesh: blk: 16 (over y, x), tp: 8 (over z, core).
Axes of the slice: x: 4, y: 4, z: 4, core: 2. Of those that a mesh axis runs over, the one named last changes fastest.
Arguments:
- hidden_in: bfloat16 [8192, 6144], P('blk', 'tp'), may hold values from -40 to 40
- ln_gain: float32 [6144], replicated, may hold values from 0.1 to 1.9
- w_qkv: bfloat16 [6144, 3, 3072], P(None, None, 'tp'), may hold values from -1 to 1
- w_out: bfloat16 [3072, 6144], P('tp'), may hold values from -0.625 to 0.625
- doc_lengths: int32 [64], replicated, may hold values from 0 to 4096, as said below
- segment_ids: int32 [8192], P('blk'), may hold values from 0 to 63, as said below
- pair_table: int32 [16, 16], replicated, may hold values from 0 to 1, as said below
- page_table: int32 [512], P('blk'), may hold values from 0 to 511, as said below
Outputs:
- attn_out: bfloat16 [8192, 6144], P('blk', 'tp')
- page_cache: bfloat16 [2, 512, 16, 3072], P(None, 'blk', None, 'tp')
The draws below stay inside these ranges and needn't reach their ends.
Inputs may be any that keep to these rules, and one draw needn't show every extreme that they name: `doc_lengths`: the 64 documents in stream order; they sum to 8192, the empty ones stand just before the last slot, which holds the stream's last document, and the second document has exactly 4096 tokens. segment_ids[t] is the number of documents that end at or before token t; the last token belongs to slot 63. pair_table[i, j] is 1 exactly where a token of block j of 512 tokens and a token at or after it in block i lie in one document. `page_table`: the 32 entries of one block of tokens are that block's own page numbers, each once.
All inputs are finite; a program needn't handle non-finite values.
Results may differ from the reference program's by a relative error of at most 0.014.
Values may be sent and summed in bfloat16 or wider, within the bound.
A program may use at most 256 MiB of HBM per device.

```python
import jax
import jax.numpy as jnp
from jax import lax

D = 6144
HEADS = 32
HD = 96
ROT = 24
PAGE = 16
TOK_DEV = 512
TOKENS = 8192
MOST = 4096
NDOCS = 64
NPAGES = 512
PG_DEV = 32
N_BLK = 16
N_TP = 8


def document_ends(key):
    base = jax.random.fold_in(key, 17)
    key_rest, key_first = jax.random.split(base)
    rest = jax.random.randint(key_rest, (NDOCS,), TOK_DEV // 4, MOST + 1, dtype=jnp.int32)
    opening_len = jax.random.randint(key_first, (), TOK_DEV // 4, MOST - TOK_DEV + 1, dtype=jnp.int32)
    opening_len = opening_len + (opening_len % TOK_DEV == 0).astype(jnp.int32)
    raw_lengths = rest.at[0].set(opening_len).at[1].set(MOST)
    capped = jnp.minimum(jnp.cumsum(raw_lengths), TOKENS).astype(jnp.int32)
    below = capped < TOKENS
    last_start = jnp.max(jnp.where(below, capped, 0)).astype(jnp.int32)
    shifted = jnp.where(below, capped, last_start).astype(jnp.int32)
    return shifted.at[NDOCS - 1].set(TOKENS).astype(jnp.int32)


def segment_numbers(key):
    doc_ends = document_ends(key)
    token_index = jnp.arange(TOKENS, dtype=jnp.int32)
    return jnp.sum((doc_ends[None, :] <= token_index[:, None]).astype(jnp.int32), axis=1).astype(jnp.int32)


def draw_doc_lengths(key, part):
    doc_ends = document_ends(key)
    earlier = jnp.concatenate([jnp.zeros((1,), jnp.int32), doc_ends[:-1]])
    return (doc_ends - earlier).astype(jnp.int32)


def draw_segment_ids(key, part):
    return segment_numbers(key)


def draw_pair_table(key, part):
    segments = segment_numbers(key)
    block_total = TOKENS // TOK_DEV
    opening = segments[::TOK_DEV]
    closing = segments[TOK_DEV - 1::TOK_DEV]
    row_ids = jnp.arange(block_total, dtype=jnp.int32)[:, None]
    col_ids = jnp.arange(block_total, dtype=jnp.int32)[None, :]
    table = (row_ids == col_ids) | (col_ids < row_ids) & (closing[None, :] == opening[:, None])
    return table.astype(jnp.int32)


def draw_page_table(key, part):
    block_total = TOKENS // TOK_DEV
    block_keys = jax.random.split(jax.random.fold_in(key, 29), block_total)
    orders = jax.vmap(lambda single: jax.random.permutation(single, PG_DEV))(block_keys).astype(jnp.int32)
    offsets = (jnp.arange(block_total, dtype=jnp.int32) * PG_DEV)[:, None]
    return (orders + offsets).reshape(NPAGES).astype(jnp.int32)


def draw_hidden_in(key, part):
    key_one = jax.random.fold_in(key, 0)
    result = jnp.clip(jax.random.normal(key_one, (TOKENS, D), jnp.float32), -6.0, 6.0)
    return result.astype(jnp.bfloat16)


def draw_w_qkv(key, part):
    key_one = jax.random.fold_in(key, 0)
    scale = D ** (-0.5)
    result = jnp.clip(jax.random.normal(key_one, (D, 3, HEADS * HD), jnp.float32), -6.0, 6.0) * scale
    return result.astype(jnp.bfloat16)


def spiked(drawn, own_key, source, target, shards_of, factor):
    owner, partner = [(jnp.arange(drawn.shape[axis_at]) // (drawn.shape[axis_at] // shards_of)).reshape([-1 if axis == axis_at else 1 for axis in range(drawn.ndim)]) for axis_at in (source, target)]
    chosen = jax.random.permutation(own_key, shards_of)[partner]
    strong = (owner == chosen) | (owner == (partner + shards_of // 2) % shards_of)
    return jnp.where(strong, factor * drawn, drawn)


def steps_of(key, extent, cuts, low, largest):
    def one(position, shards_of):
        heights = jax.random.uniform(jax.random.fold_in(jax.random.fold_in(key, 6), position), (shards_of,), jnp.float32, low / len(cuts), largest / len(cuts))
        return jnp.repeat(jnp.exp(heights), extent[position] // shards_of).reshape((-1,) + (1,) * (len(extent) - position - 1))

    factor_of = one(*cuts[0])
    for cut in cuts[1:]:
        factor_of = factor_of * one(*cut)
    return factor_of


def noise_with(own_key, extent, spread, most, cuts, heavy, kind=jnp.bfloat16):
    values = spread * jax.random.normal(own_key, extent, jnp.float32)
    if cuts:
        values = values * steps_of(own_key, extent, cuts, -0.22, 0.18)
    return jnp.clip(spiked(values, jax.random.fold_in(own_key, 3), *heavy), -most, most).astype(kind)


def setup_inputs(seed: int = 0) -> dict:
    splits = jax.random.split(jax.random.key(seed), 9)
    return {
        "hidden_in": draw_hidden_in(jax.random.fold_in(splits[8], 71), 0),
        "ln_gain": jnp.clip(1.0 + 0.18 * jax.random.normal(splits[1], (D,), jnp.float32), 0.1, 1.9),
        "w_qkv": draw_w_qkv(jax.random.fold_in(splits[8], 71), 0),
        "w_out": noise_with(splits[3], (HEADS * HD, D), (HEADS * HD // 16) ** -0.5, 0.625, ((0, 8),), (0, 1, 8, 2.0)),
        "doc_lengths": draw_doc_lengths(jax.random.fold_in(splits[8], 71), 0),
        "segment_ids": draw_segment_ids(jax.random.fold_in(splits[8], 71), 0),
        "pair_table": draw_pair_table(jax.random.fold_in(splits[8], 71), 0),
        "page_table": draw_page_table(jax.random.fold_in(splits[8], 71), 0),
    }


EPSILON = 1e-05

def layer_norm(hidden_in, ln_gain):
    values32 = hidden_in.astype(jnp.float32)
    row_mean = lax.optimization_barrier(jnp.mean(values32, axis=-1, keepdims=True))
    centred = values32 - row_mean
    row_var = lax.optimization_barrier(jnp.mean(centred * centred, axis=-1, keepdims=True))
    return (centred * lax.rsqrt(row_var + EPSILON) * ln_gain).astype(jnp.bfloat16)

def doc_positions(token_index, doc_lengths, segment_ids):
    starts = (jnp.cumsum(doc_lengths) - doc_lengths).astype(jnp.int32)
    slots = jnp.arange(doc_lengths.shape[0], dtype=jnp.int32)
    in_document = segment_ids[:, None] == slots[None, :]
    offsets = lax.optimization_barrier(jnp.sum(jnp.where(in_document, starts[None, :], 0), axis=1)).astype(jnp.int32)
    return (token_index - offsets).astype(jnp.int32)

def rotary(head_block, positions):
    half_rot = ROT // 2
    frequency = 10000.0 ** (-(2.0 * jnp.arange(half_rot, dtype=jnp.float32)) / ROT)
    angles = positions.astype(jnp.float32)[:, None] * frequency[None, :]
    cosine = jnp.cos(angles)[:, None, :]
    sine_part = jnp.sin(angles)[:, None, :]
    lower_half = head_block[..., :half_rot]
    upper_half = head_block[..., half_rot:ROT]
    return jnp.concatenate([lower_half * cosine - upper_half * sine_part, upper_half * cosine + lower_half * sine_part, head_block[..., ROT:]], axis=-1)

def attention(queries, key_rows, values, segment_ids, pair_table):
    reach = N_BLK // 2
    window = (reach + 1) * TOK_DEV
    scale = HD ** (-0.5)

    def one_block(block_id):
        q_start = block_id * TOK_DEV
        k_start = jnp.maximum(block_id - reach, 0) * TOK_DEV
        q_part = lax.dynamic_slice_in_dim(queries, q_start, TOK_DEV, 0).astype(jnp.float32)
        k_part = lax.dynamic_slice_in_dim(key_rows, k_start, window, 0).astype(jnp.float32)
        v_part = lax.dynamic_slice_in_dim(values, k_start, window, 0).astype(jnp.float32)
        q_seg = lax.dynamic_slice_in_dim(segment_ids, q_start, TOK_DEV, 0)
        k_seg = lax.dynamic_slice_in_dim(segment_ids, k_start, window, 0)
        q_index = q_start + jnp.arange(TOK_DEV, dtype=jnp.int32)
        k_index = k_start + jnp.arange(window, dtype=jnp.int32)
        table_row = lax.dynamic_index_in_dim(pair_table, block_id, 0, keepdims=False)
        live = jnp.take(table_row, k_index // TOK_DEV)
        allowed = (live[None, :] > 0) & (q_seg[:, None] == k_seg[None, :]) & (k_index[None, :] <= q_index[:, None])
        scores = jnp.einsum('qhd,khd->hqk', q_part, k_part) * scale
        scores = jnp.where(allowed[None], scores, -jnp.inf)
        peak = lax.optimization_barrier(jnp.max(scores, axis=-1, keepdims=True))
        weights = jnp.exp(scores - peak)
        totals = lax.optimization_barrier(jnp.sum(weights, axis=-1))
        rounded = lax.optimization_barrier(weights.astype(jnp.bfloat16)).astype(jnp.float32)
        mixed = jnp.einsum('hqk,khd->qhd', rounded, v_part) / jnp.transpose(totals)[:, :, None]
        return mixed.astype(jnp.bfloat16)
    blocks = lax.map(one_block, jnp.arange(N_BLK, dtype=jnp.int32))
    return blocks.reshape(TOKENS, HEADS * HD)

def reference(hidden_in, ln_gain, w_qkv, w_out, doc_lengths, segment_ids, pair_table, page_table):
    normed = layer_norm(hidden_in, ln_gain)
    projected = jnp.dot(normed, w_qkv.reshape(D, 3 * HEADS * HD), preferred_element_type=jnp.float32).reshape(TOKENS, 3, HEADS, HD)
    token_index = jnp.arange(TOKENS, dtype=jnp.int32)
    positions = doc_positions(token_index, doc_lengths, segment_ids)
    queries = rotary(projected[:, 0], positions).astype(jnp.bfloat16)
    key_rows = rotary(projected[:, 1], positions).astype(jnp.bfloat16)
    values = projected[:, 2].astype(jnp.bfloat16)
    heads_out = attention(queries, key_rows, values, segment_ids, pair_table)
    group_cols = HEADS * HD // N_TP
    summed = jnp.zeros((TOKENS, D), jnp.float32)
    for group_id in range(N_TP):
        partial_term = jnp.dot(heads_out[:, group_id * group_cols:(group_id + 1) * group_cols], w_out[group_id * group_cols:(group_id + 1) * group_cols], preferred_element_type=jnp.float32)
        summed = summed + lax.optimization_barrier(partial_term.astype(jnp.bfloat16)).astype(jnp.float32)
    attn_out = summed.astype(jnp.bfloat16)
    stacked = jnp.stack([key_rows.reshape(NPAGES, PAGE, HEADS * HD), values.reshape(NPAGES, PAGE, HEADS * HD)])
    page_cache = jnp.zeros_like(stacked).at[:, page_table].set(stacked)
    return (attn_out, page_cache)
```

```python
import functools

import jax
import jax.numpy as jnp
from jax import lax
from jax.experimental import pallas as pl
from jax.experimental.pallas import tpu as pltpu
from jax.sharding import PartitionSpec as P

HD = 96
ROT = 24
PAGE = 16
ROWS = 512
HALF = 256
SHARD = 768
COLS = 384
EPSILON = 1e-05
LOG2E = 1.4426950408889634
MESH = pl.DeviceIdType.MESH


def remote(src, dst, send, recv, where):
    return pltpu.make_async_remote_copy(
        src_ref=src, dst_ref=dst, send_sem=send, recv_sem=recv, device_id=where, device_id_type=MESH
    )


def project_kernel(
    hid_ref, gain_ref, table_ref, w_ref, out_ref,
    gathered, wbuf, acc, stats, columns, normed,
    w_sem, own_sem, stat_send, stat_recv, ici_send, ici_recv, sib_send, sib_recv,
):
    b = lax.axis_index("blk")
    t = lax.axis_index("tp")
    z, c = t // 2, t % 2
    sibling = (b, z * 2 + 1 - c)
    after = (b, ((z + 1) % 4) * 2 + c)
    before = (b, ((z + 3) % 4) * 2 + c)

    def origin(dz, k):
        return ((z + dz + 4) % 4) * 2 + (c + k) % 2

    order = [(0, 0), (0, 1), (3, 0), (1, 0), (3, 1), (1, 1), (2, 0), (2, 1)]
    loads = []
    for i, (dz, k) in enumerate(order):
        rows = pl.ds(pl.multiple_of(origin(dz, k) * SHARD, SHARD), SHARD)
        copy = pltpu.make_async_copy(w_ref.at[:, rows, :], wbuf.at[:, rows, :], w_sem.at[i])
        copy.start()
        loads.append(copy)
    own_copy = pltpu.make_async_copy(hid_ref, gathered.at[t], own_sem)
    own_copy.start()

    x = hid_ref[...].astype(jnp.float32)
    mean = jnp.sum(x, axis=1, keepdims=True) * (1.0 / SHARD)
    centred = x - mean
    spread = jnp.sum(centred * centred, axis=1, keepdims=True)
    lane = lax.broadcasted_iota(jnp.int32, (ROWS, 128), 1)
    both = jnp.where(lane == 0, mean, spread)
    stats[t] = jnp.transpose(both)[:8]

    barrier = pltpu.get_barrier_semaphore()
    for d in range(1, 8):
        pl.semaphore_signal(barrier, inc=1, device_id=(b, (t + d) % 8), device_id_type=MESH)
    pl.semaphore_wait(barrier, 7)

    a_rows, b_rows = pl.ds(0, HALF), pl.ds(HALF, HALF)

    def piece(who, rows):
        return gathered.at[who, rows]

    stat_copies = []
    for d in range(1, 8):
        copy = remote(stats.at[t], stats.at[t], stat_send.at[d - 1], stat_recv.at[d - 1], (b, (t + d) % 8))
        copy.start()
        stat_copies.append(copy)
    plus = [
        remote(hid_ref.at[a_rows], piece(t, a_rows), ici_send.at[0], ici_recv.at[0], after),
        remote(hid_ref.at[b_rows], piece(t, b_rows), ici_send.at[1], ici_recv.at[1], after),
        remote(piece(origin(3, 0), a_rows), piece(origin(3, 0), a_rows), ici_send.at[2], ici_recv.at[2], after),
    ]
    minus = [
        remote(hid_ref.at[b_rows], piece(t, b_rows), ici_send.at[3], ici_recv.at[3], before),
        remote(hid_ref.at[a_rows], piece(t, a_rows), ici_send.at[4], ici_recv.at[4], before),
        remote(piece(origin(1, 0), b_rows), piece(origin(1, 0), b_rows), ici_send.at[5], ici_recv.at[5], before),
    ]
    across = [remote(hid_ref, gathered.at[t], sib_send.at[0], sib_recv.at[0], sibling)]
    for i, (dz, rows) in enumerate(
        [(3, a_rows), (1, b_rows), (3, b_rows), (1, a_rows), (2, a_rows), (2, b_rows)]
    ):
        who = origin(dz, 0)
        across.append(remote(piece(who, rows), piece(who, rows), sib_send.at[i + 1], sib_recv.at[i + 1], sibling))
    plus[0].start()
    minus[0].start()
    across[0].start()
    plus[1].start()
    minus[1].start()

    acc[...] = jnp.zeros_like(acc)
    for copy in stat_copies:
        copy.wait_recv()
    means = stats[:, 0, :]
    whole_mean = jnp.sum(means, axis=0, keepdims=True) * 0.125
    off = means - whole_mean
    total = jnp.sum(stats[:, 1, :], axis=0, keepdims=True) + SHARD * jnp.sum(off * off, axis=0, keepdims=True)
    inverse = lax.rsqrt(total * (1.0 / (8 * SHARD)) + EPSILON)
    columns[0] = jnp.transpose(jnp.broadcast_to(whole_mean, (128, ROWS)))
    columns[1] = jnp.transpose(jnp.broadcast_to(inverse, (128, ROWS)))

    def compute(who, half):
        start = half * HALF

        def normalise(i, carry):
            rows = pl.ds(pl.multiple_of(start + i * 64, 64), 64)
            here = pl.ds(pl.multiple_of(i * 64, 64), 64)
            centre, scale = columns[0, rows, :], columns[1, rows, :]
            for j in range(SHARD // 128):
                span = slice(128 * j, 128 * j + 128)
                value = gathered[who, rows, span].astype(jnp.float32)
                gain = gain_ref[who, :, span]
                normed[here, span] = ((value - centre) * scale * gain).astype(jnp.bfloat16)
            return carry

        lax.fori_loop(0, HALF // 64, normalise, 0)
        rows = pl.ds(start, HALF)
        depth = pl.ds(pl.multiple_of(who * SHARD, SHARD), SHARD)

        def multiply(kind, carry):
            acc[kind, rows, :] += jnp.dot(
                normed[...], wbuf[kind, depth, :], preferred_element_type=jnp.float32
            )
            return carry

        lax.fori_loop(0, 3, multiply, 0)

    own_copy.wait()
    loads[0].wait()
    compute(t, 0)
    compute(t, 1)
    loads[1].wait()
    across[0].wait_recv()
    compute(origin(0, 1), 0)
    compute(origin(0, 1), 1)

    plus[0].wait_recv()
    plus[2].start()
    across[1].start()
    minus[0].wait_recv()
    minus[2].start()
    across[2].start()
    loads[2].wait()
    compute(origin(3, 0), 0)
    loads[3].wait()
    compute(origin(1, 0), 1)
    loads[4].wait()
    across[1].wait_recv()
    compute(origin(3, 1), 0)
    loads[5].wait()
    across[2].wait_recv()
    compute(origin(1, 1), 1)

    plus[1].wait_recv()
    across[3].start()
    minus[1].wait_recv()
    across[4].start()
    compute(origin(3, 0), 1)
    compute(origin(1, 0), 0)
    across[3].wait_recv()
    compute(origin(3, 1), 1)
    across[4].wait_recv()
    compute(origin(1, 1), 0)

    plus[2].wait_recv()
    across[5].start()
    minus[2].wait_recv()
    across[6].start()
    loads[6].wait()
    compute(origin(2, 0), 0)
    compute(origin(2, 0), 1)
    loads[7].wait()
    across[5].wait_recv()
    compute(origin(2, 1), 0)
    across[6].wait_recv()
    compute(origin(2, 1), 1)

    cosine, sine = table_ref[0], table_ref[1]
    for kind in range(3):
        turned = jnp.transpose(acc[kind])
        for h in range(COLS // HD):
            part = turned[h * HD:(h + 1) * HD]
            if kind < 2:
                head = part[:ROT]
                swapped = jnp.concatenate([head[ROT // 2:], head[:ROT // 2]], axis=0)
                part = jnp.concatenate([head * cosine + swapped * sine, part[ROT:]], axis=0)
            out_ref[h, kind] = part.astype(jnp.bfloat16)

    for copy in stat_copies + plus + minus + across:
        copy.wait_send()


def attend_kernel(
    qkv_ref, low_ref, dest_ref, out_ref, page_ref,
    qbuf, kv, keys, peak, total, acc, done,
    own_sem, kv_send, kv_recv, q_send, q_recv, ag_send, ag_recv, o_send, o_recv,
):
    b = lax.axis_index("blk")
    t = lax.axis_index("tp")
    y, x, c = b // 4, b % 4, t % 2
    mine = (1 - c) * y + c * x
    group = (1 - c) * x + c * y

    def block_of(a, g):
        return (1 - c) * (a * 4 + g) + c * (g * 4 + a)

    barrier = pltpu.get_barrier_semaphore()
    for d in range(1, 4):
        for where in (block_of((mine + d) % 4, group), block_of(mine, (group + d) % 4)):
            pl.semaphore_signal(barrier, inc=1, device_id=(where, t), device_id_type=MESH)
    pl.semaphore_wait(barrier, 6)

    both = pl.ds(1, 2)
    kept = pltpu.make_async_copy(qkv_ref.at[mine, both], kv.at[group, mine], own_sem.at[0])
    kept_q = pltpu.make_async_copy(qkv_ref.at[mine, 0], qbuf.at[mine], own_sem.at[1])
    kept.start()
    kept_q.start()
    sends, q_copies, kv_copies = [], [], []
    order = (1, 3, 2)
    for d in order:
        head = (mine + d) % 4
        copy = remote(
            qkv_ref.at[head, both], kv.at[group, mine], kv_send.at[d - 1], kv_recv.at[d - 1],
            (block_of(head, group), t),
        )
        copy.start()
        kv_copies.append(copy)
    ag_copies = []
    for d in order:
        copy = remote(
            qkv_ref.at[mine, both], kv.at[group, mine], ag_send.at[0, d - 1], ag_recv.at[0, d - 1],
            (block_of(mine, (group + d) % 4), t),
        )
        copy.start()
        ag_copies.append(copy)
    for d in order:
        head = (mine + d) % 4
        copy = remote(
            qkv_ref.at[head, 0], qbuf.at[mine], q_send.at[d - 1], q_recv.at[d - 1],
            (block_of(head, group), t),
        )
        copy.start()
        q_copies.append(copy)

    for d, arrived in zip(order, kv_copies):
        arrived.wait_recv()
        slot = (mine + 4 - d) % 4
        for e in order:
            copy = remote(
                kv.at[group, slot], kv.at[group, slot], ag_send.at[d, e - 1], ag_recv.at[d, e - 1],
                (block_of(mine, (group + e) % 4), t),
            )
            copy.start()
            ag_copies.append(copy)

    spots = lax.broadcasted_iota(jnp.int32, (ROWS, ROWS), 0)
    chosen = (spots == dest_ref[...]).astype(jnp.float32).astype(jnp.bfloat16)
    for kind in range(2):
        source = jnp.concatenate([qkv_ref[h, kind + 1] for h in range(4)], axis=0)
        page_ref[kind] = lax.dot_general(
            chosen, source, (((1,), (1,)), ((), ())), preferred_element_type=jnp.float32
        ).astype(jnp.bfloat16)

    kept.wait()
    kept_q.wait()
    for copy in q_copies + ag_copies:
        copy.wait_recv()

    def turn(i, carry):
        keys[i // 4, i % 4] = jnp.transpose(kv[i // 4, i % 4, 0].astype(jnp.float32)).astype(jnp.bfloat16)
        return carry

    lax.fori_loop(0, 16, turn, 0)

    factor = LOG2E * HD ** (-0.5)
    depth_index = lax.broadcasted_iota(jnp.int32, (ROWS, ROWS), 0)
    o_copies = []
    for step in range(4):
        slot = (mine + 1 + step) % 4
        query_block = block_of(slot, group)
        low = low_ref[query_block]
        query = qbuf[slot]

        def attend(key_block, first):
            a = (1 - c) * (key_block // 4) + c * (key_block % 4)
            g = (1 - c) * (key_block % 4) + c * (key_block // 4)
            score = jnp.dot(keys[g, a], query, preferred_element_type=jnp.float32)
            allowed = depth_index >= low - key_block * ROWS
            if first:
                allowed = allowed & (depth_index <= lax.broadcasted_iota(jnp.int32, (ROWS, ROWS), 1))
            score = jnp.where(allowed, score, -1e30)
            highest = jnp.max(score, axis=0, keepdims=True)
            if not first:
                highest = jnp.maximum(highest, peak[...])
            weight = jnp.exp2((score - highest) * factor)
            added = jnp.sum(weight, axis=0, keepdims=True)
            mixed = jnp.dot(kv[g, a, 1], weight.astype(jnp.bfloat16), preferred_element_type=jnp.float32)
            if first:
                total[...] = added
                acc[...] = mixed
            else:
                fade = jnp.exp2((peak[...] - highest) * factor)
                total[...] = total[...] * fade + added
                acc[...] = acc[...] * fade + mixed
            peak[...] = highest

        attend(query_block, True)

        def older(r, carry):
            key_block = query_block - 1 - r

            @pl.when(key_block >= 0)
            def _():
                attend(key_block, False)

            return carry

        lax.fori_loop(0, 8, older, 0)
        result = (acc[...] / total[...]).astype(jnp.bfloat16)
        if step < 3:
            done[slot] = result
            copy = remote(
                done.at[slot], out_ref.at[mine], o_send.at[step], o_recv.at[step], (block_of(slot, group), t)
            )
            copy.start()
            o_copies.append(copy)
        else:
            out_ref[mine] = result

    for copy in o_copies:
        copy.wait_recv()
    for copy in kv_copies + q_copies + ag_copies + o_copies:
        copy.wait_send()


def output_kernel(
    o_ref, w_ref, out_ref,
    wbuf, x, sib_out, sib_in, tx, rx, w_sem, sib_send, sib_recv, send, recv,
):
    b = lax.axis_index("blk")
    t = lax.axis_index("tp")
    z, c = t // 2, t % 2
    sibling = (b, z * 2 + 1 - c)
    after = (b, ((z + 1) % 4) * 2 + c)
    before = (b, ((z + 3) % 4) * 2 + c)
    order = (2, 1, 3, 0)

    def owner(dz, k):
        return ((z + dz) % 4) * 2 + (c + k) % 2

    loads = {}
    for i, key in enumerate([(2, 1), (2, 0), (1, 1), (1, 0), (3, 1), (3, 0), (0, 1), (0, 0)]):
        who = owner(*key)
        span = pl.ds(pl.multiple_of(who * SHARD, SHARD), SHARD)
        loads[key] = pltpu.make_async_copy(w_ref.at[:, span], wbuf.at[who], w_sem.at[i])
        loads[key].start()

    barrier = pltpu.get_barrier_semaphore()
    for where in (sibling, after, before):
        pl.semaphore_signal(barrier, inc=1, device_id=where, device_id_type=MESH)

    flat = jnp.concatenate([o_ref[h] for h in range(4)], axis=0).astype(jnp.float32)
    x[...] = jnp.transpose(flat).astype(jnp.bfloat16)
    pl.semaphore_wait(barrier, 3)

    a_rows, b_rows = slice(0, HALF), slice(HALF, ROWS)

    def product(key, rows):
        return jnp.dot(x[rows, :], wbuf[owner(*key)], preferred_element_type=jnp.float32)

    across = []

    def give(i):
        loads[(order[i], 1)].wait()
        for rows in (a_rows, b_rows):
            sib_out[i, rows, :] = product((order[i], 1), rows).astype(jnp.bfloat16)
        copy = remote(sib_out.at[i], sib_in.at[i], sib_send.at[i], sib_recv.at[i], sibling)
        copy.start()
        across.append(copy)

    def own(i, rows):
        return product((order[i], 0), rows) + sib_in[i, rows, :].astype(jnp.float32)

    def leave(i, rows, target):
        k = 2 * i + (0 if rows is a_rows else 1)
        copy = remote(tx.at[i, rows], rx.at[i, rows], send.at[k], recv.at[k], target)
        copy.start()
        return copy

    give(0)
    give(1)
    loads[(2, 0)].wait()
    across[0].wait_recv()
    tx[0, a_rows, :] = own(0, a_rows).astype(jnp.bfloat16)
    far_a = leave(0, a_rows, after)
    tx[0, b_rows, :] = own(0, b_rows).astype(jnp.bfloat16)
    far_b = leave(0, b_rows, before)
    give(2)
    loads[(1, 0)].wait()
    across[1].wait_recv()
    tx[1, b_rows, :] = own(1, b_rows).astype(jnp.bfloat16)
    next_b = leave(1, b_rows, after)
    loads[(3, 0)].wait()
    across[2].wait_recv()
    tx[2, a_rows, :] = own(2, a_rows).astype(jnp.bfloat16)
    prev_a = leave(2, a_rows, before)
    far_a.wait_recv()
    tx[1, a_rows, :] = (own(1, a_rows) + rx[0, a_rows, :].astype(jnp.float32)).astype(jnp.bfloat16)
    next_a = leave(1, a_rows, after)
    far_b.wait_recv()
    tx[2, b_rows, :] = (own(2, b_rows) + rx[0, b_rows, :].astype(jnp.float32)).astype(jnp.bfloat16)
    prev_b = leave(2, b_rows, before)
    give(3)
    loads[(0, 0)].wait()
    across[3].wait_recv()
    next_b.wait_recv()
    prev_a.wait_recv()
    next_a.wait_recv()
    prev_b.wait_recv()
    for rows in (a_rows, b_rows):
        whole = own(3, rows) + rx[1, rows, :].astype(jnp.float32) + rx[2, rows, :].astype(jnp.float32)
        out_ref[rows, :] = whole.astype(jnp.bfloat16)
    for copy in across + [far_a, far_b, next_a, next_b, prev_a, prev_b]:
        copy.wait_send()


VMEM = pl.BlockSpec(memory_space=pltpu.VMEM)
ANY = pl.BlockSpec(memory_space=pl.ANY)
DMA = pltpu.SemaphoreType.DMA


def params(number):
    return pltpu.CompilerParams(
        collective_id=number, has_side_effects=True, vmem_limit_bytes=60 * 1024 * 1024
    )


def per_device(hidden_in, ln_gain, w_qkv, w_out, doc_lengths, segment_ids, pair_table, page_table):
    b = lax.axis_index("blk")
    bf16, f32 = jnp.bfloat16, jnp.float32
    starts = jnp.cumsum(doc_lengths) - doc_lengths
    tokens = jnp.arange(16 * ROWS, dtype=jnp.int32)
    low = jnp.max(jnp.where(starts[:, None] <= tokens[None, :], starts[:, None], 0), axis=0)
    low = low.reshape(16, 1, ROWS)
    mine = jnp.arange(ROWS, dtype=jnp.int32)
    positions = b * ROWS + mine - lax.dynamic_index_in_dim(low, b, 0, keepdims=False)[0]
    frequency = 10000.0 ** (-(2.0 * jnp.arange(ROT // 2, dtype=f32)) / ROT)
    angles = frequency[:, None] * positions.astype(f32)[None, :]
    cosine, sine = jnp.cos(angles), jnp.sin(angles)
    table = jnp.stack([jnp.concatenate([cosine, cosine]), jnp.concatenate([-sine, sine])])
    local_pages = page_table - b * (ROWS // PAGE)
    dest = (local_pages[:, None] * PAGE + jnp.arange(PAGE, dtype=jnp.int32)[None, :]).reshape(1, ROWS)

    qkv = pl.pallas_call(
        project_kernel,
        out_shape=jax.ShapeDtypeStruct((4, 3, HD, ROWS), bf16),
        in_specs=[VMEM, VMEM, VMEM, ANY],
        out_specs=VMEM,
        scratch_shapes=[
            pltpu.VMEM((8, ROWS, SHARD), bf16),
            pltpu.VMEM((3, 8 * SHARD, COLS), bf16),
            pltpu.VMEM((3, ROWS, COLS), f32),
            pltpu.VMEM((8, 8, ROWS), f32),
            pltpu.VMEM((2, ROWS, 128), f32),
            pltpu.VMEM((HALF, SHARD), bf16),
            DMA((8,)), DMA, DMA((7,)), DMA((7,)), DMA((6,)), DMA((6,)), DMA((7,)), DMA((7,)),
        ],
        compiler_params=params(0),
        name="project",
    )(hidden_in, ln_gain.reshape(8, 1, SHARD), table, jnp.transpose(w_qkv, (1, 0, 2)))

    heads, pages = pl.pallas_call(
        attend_kernel,
        out_shape=(
            jax.ShapeDtypeStruct((4, HD, ROWS), bf16),
            jax.ShapeDtypeStruct((2, ROWS, COLS), bf16),
        ),
        in_specs=[VMEM, VMEM, VMEM],
        out_specs=(VMEM, VMEM),
        scratch_shapes=[
            pltpu.VMEM((4, HD, ROWS), bf16),
            pltpu.VMEM((4, 4, 2, HD, ROWS), bf16),
            pltpu.VMEM((4, 4, ROWS, HD), bf16),
            pltpu.VMEM((1, ROWS), f32),
            pltpu.VMEM((1, ROWS), f32),
            pltpu.VMEM((HD, ROWS), f32),
            pltpu.VMEM((4, HD, ROWS), bf16),
            DMA((2,)), DMA((3,)), DMA((3,)), DMA((3,)), DMA((3,)),
            DMA((4, 3)), DMA((4, 3)), DMA((3,)), DMA((3,)),
        ],
        compiler_params=params(1),
        name="attend",
    )(qkv, low, dest)

    attn_out = pl.pallas_call(
        output_kernel,
        out_shape=jax.ShapeDtypeStruct((ROWS, SHARD), bf16),
        in_specs=[VMEM, ANY],
        out_specs=VMEM,
        scratch_shapes=[
            pltpu.VMEM((8, COLS, SHARD), bf16),
            pltpu.VMEM((ROWS, COLS), bf16),
            pltpu.VMEM((4, ROWS, SHARD), bf16),
            pltpu.VMEM((4, ROWS, SHARD), bf16),
            pltpu.VMEM((3, ROWS, SHARD), bf16),
            pltpu.VMEM((3, ROWS, SHARD), bf16),
            DMA((8,)), DMA((4,)), DMA((4,)), DMA((6,)), DMA((6,)),
        ],
        compiler_params=params(2),
        name="output",
    )(heads, w_out)
    return attn_out, pages.reshape(2, ROWS // PAGE, PAGE, COLS)


def solution(mesh):
    placed = (P("blk", "tp"), P(), P(None, None, "tp"), P("tp", None), P(), P("blk"), P(), P("blk"))
    return jax.shard_map(
        per_device,
        mesh=mesh,
        in_specs=placed,
        out_specs=(P("blk", "tp"), P(None, "blk", None, "tp")),
        check_vma=False,
    )
```

```python
import jax
import jax.numpy as jnp
import numpy as np
from jax import lax
from jax.experimental import pallas as pl
from jax.experimental.pallas import tpu as pltpu
from jax.sharding import PartitionSpec as P

HD = 96
ROT = 24
PAGE = 16
ROWS = 512
HALF = 256
QUARTER = 128
SHARD = 768
COLS = 384
EPSILON = 1e-05
FACTOR = 1.4426950408889634 * HD ** (-0.5)
LOWEST = -1e30
MESH = pl.DeviceIdType.MESH
F32, BF16 = jnp.float32, jnp.bfloat16


def remote(src, dst, send, recv, where):
    return pltpu.make_async_remote_copy(
        src_ref=src, dst_ref=dst, send_sem=send, recv_sem=recv, device_id=where, device_id_type=MESH
    )


def iota(shape, axis):
    return lax.broadcasted_iota(jnp.int32, shape, axis)


def layer_kernel(
    hid_ref, gain_ref, lens_ref, pages_ref, freq_ref, wqkv_ref, wout_ref,
    out_ref, page_ref,
    gathered, wbuf, acc, stats, columns, normed, table, qkv, qbuf, kv, keys, lows,
    peak, total, mix, done, heads, wo, x, sib_out, sib_in, tx, rx, hold, far_hold,
    w_sem, wo_sem, own_sem, stat_send, stat_recv, ici_send, ici_recv, sib_send, sib_recv,
    keep_sem, kv_send, kv_recv, q_send, q_recv, ag_send, ag_recv, o_send, o_recv,
    give_send, give_recv, ring_send, ring_recv,
):
    b = lax.axis_index("blk")
    t = lax.axis_index("tp")
    z, c = t // 2, t % 2
    y, xx = b // 4, b % 4
    sibling = (b, z * 2 + 1 - c)
    after = (b, ((z + 1) % 4) * 2 + c)
    before = (b, ((z + 3) % 4) * 2 + c)
    mine = (1 - c) * y + c * xx
    group = (1 - c) * xx + c * y
    order = (1, 3, 2)

    def block_of(a, g):
        return (1 - c) * (a * 4 + g) + c * (g * 4 + a)

    def origin(dz, k):
        return ((z + dz) % 4) * 2 + (c + k) % 2

    shard_order = [(0, 0), (0, 1), (3, 0), (1, 0), (3, 1), (1, 1), (2, 0), (2, 1)]
    loads = {}
    for i, key in enumerate(shard_order):
        rows = pl.ds(pl.multiple_of(origin(*key) * SHARD, SHARD), SHARD)
        loads[key] = pltpu.make_async_copy(wqkv_ref.at[:, rows, :], wbuf.at[:, rows, :], w_sem.at[i])
        loads[key].start()
    own_copy = pltpu.make_async_copy(hid_ref, gathered.at[t], own_sem)
    own_copy.start()
    out_loads = {}
    for i, key in enumerate([(2, 1), (2, 0), (1, 1), (1, 0), (3, 1), (3, 0), (0, 1), (0, 0)]):
        who = origin(*key)
        span = pl.ds(pl.multiple_of(who * SHARD, SHARD), SHARD)
        out_loads[key] = pltpu.make_async_copy(wout_ref.at[:, span], wo.at[who], wo_sem.at[i])
        out_loads[key].start()

    barrier = pltpu.get_barrier_semaphore()
    for d in range(1, 8):
        pl.semaphore_signal(barrier, inc=1, device_id=(b, (t + d) % 8), device_id_type=MESH)
    for d in range(1, 4):
        for where in (block_of((mine + d) % 4, group), block_of(mine, (group + d) % 4)):
            pl.semaphore_signal(barrier, inc=1, device_id=(where, t), device_id_type=MESH)

    value = hid_ref[...].astype(F32)
    mean = jnp.sum(value, axis=1, keepdims=True) * (1.0 / SHARD)
    centred = value - mean
    spread = jnp.sum(centred * centred, axis=1, keepdims=True)
    stats[t] = jnp.transpose(jnp.where(iota((ROWS, 128), 1) == 0, mean, spread))[:8]
    pl.semaphore_wait(barrier, 13)

    stat_copies = []
    for d in range(1, 8):
        copy = remote(stats.at[t], stats.at[t], stat_send.at[d - 1], stat_recv.at[d - 1], (b, (t + d) % 8))
        copy.start()
        stat_copies.append(copy)

    def part(half, k):
        return pl.ds(half * HALF + k * QUARTER, QUARTER)

    plus, minus, across = [], [], []
    for half in range(2):
        q0, q1 = part(half, 0), part(half, 1)
        both = pl.ds(half * HALF, HALF)
        left, right, far = origin(3, 0), origin(1, 0), origin(2, 0)

        def ici(i, who, rows, src, where):
            return remote(src.at[rows], gathered.at[who, rows], ici_send.at[half, i], ici_recv.at[half, i], where)

        plus.append([
            ici(0, t, q0, hid_ref, after), ici(1, t, q1, hid_ref, after), ici(2, left, q0, gathered.at[left], after),
        ])
        minus.append([
            ici(3, t, q1, hid_ref, before), ici(4, t, q0, hid_ref, before), ici(5, right, q1, gathered.at[right], before),
        ])
        moved = [(t, both), (left, q0), (right, q1), (left, q1), (right, q0), (far, q0), (far, q1)]
        across.append([
            remote(
                (hid_ref if i == 0 else gathered.at[who]).at[rows], gathered.at[who, rows],
                sib_send.at[half, i], sib_recv.at[half, i], sibling,
            )
            for i, (who, rows) in enumerate(moved)
        ])

    def send_own(half):
        plus[half][0].start()
        minus[half][0].start()
        across[half][0].start()
        plus[half][1].start()
        minus[half][1].start()

    send_own(0)

    lens = lens_ref[...].astype(F32)
    earlier = iota((64, 64), 1) < iota((64, 64), 0)
    starts = jnp.sum(jnp.where(earlier, lens, 0.0), axis=1, keepdims=True)

    def lowest(block, half):
        token = (block * ROWS + half * HALF + iota((1, HALF), 1)).astype(F32)
        return token, jnp.max(jnp.where(starts <= token, starts, 0.0), axis=0, keepdims=True)

    for half in range(2):
        token, low = lowest(b, half)
        angle = freq_ref[:, 0:1] * (token - low)
        table[half, 0] = jnp.cos(angle)
        table[half, 1] = jnp.where(iota((ROT, HALF), 0) < ROT // 2, -1.0, 1.0) * jnp.sin(angle)
        for slot in range(4):
            lows[half, slot] = lowest(block_of(slot, group), half)[1]

    for copy in stat_copies:
        copy.wait_recv()
    means = stats[:, 0, :]
    whole_mean = jnp.sum(means, axis=0, keepdims=True) * 0.125
    off = means - whole_mean
    squares = jnp.sum(stats[:, 1, :], axis=0, keepdims=True) + SHARD * jnp.sum(off * off, axis=0, keepdims=True)
    inverse = lax.rsqrt(squares * (1.0 / (8 * SHARD)) + EPSILON)
    columns[0] = jnp.transpose(jnp.broadcast_to(whole_mean, (128, ROWS)))
    columns[1] = jnp.transpose(jnp.broadcast_to(inverse, (128, ROWS)))

    def compute(key, half):
        who = origin(*key)

        def normalise(i, carry):
            rows = pl.ds(pl.multiple_of(half * HALF + i * 64, 64), 64)
            here = pl.ds(pl.multiple_of(i * 64, 64), 64)
            centre, scale = columns[0, rows, :], columns[1, rows, :]
            for j in range(SHARD // 128):
                span = slice(128 * j, 128 * j + 128)
                normed[here, span] = (
                    (gathered[who, rows, span].astype(F32) - centre) * scale * gain_ref[who, :, span]
                ).astype(BF16)
            return carry

        lax.fori_loop(0, HALF // 64, normalise, 0)
        depth = pl.ds(pl.multiple_of(who * SHARD, SHARD), SHARD)
        fresh = key == (0, 0)

        def multiply(kind, carry):
            product = jnp.dot(normed[...], wbuf[kind, depth, :], preferred_element_type=F32)
            if fresh:
                acc[kind] = product
            else:
                acc[kind] += product
            return carry

        lax.fori_loop(0, 3, multiply, 0)

    def epilogue(half):
        cosine, sine = table[half, 0], table[half, 1]
        for kind in range(3):
            turned = jnp.transpose(acc[kind])
            for h in range(COLS // HD):
                piece = turned[h * HD:(h + 1) * HD]
                if kind < 2:
                    top = piece[:ROT]
                    swapped = jnp.concatenate([top[ROT // 2:], top[:ROT // 2]], axis=0)
                    piece = jnp.concatenate([top * cosine + swapped * sine, piece[ROT:]], axis=0)
                qkv[half, h, kind] = piece.astype(BF16)

    pair = pl.ds(1, 2)
    kept, kv_copies, q_copies, ag_copies = [[], []], [[], []], [[], []], [[], []]

    def redistribute(half):
        copy = pltpu.make_async_copy(qkv.at[half, mine, pair], kv.at[half, group, mine], keep_sem.at[half, 0])
        copy.start()
        kept[half].append(copy)
        copy = pltpu.make_async_copy(qkv.at[half, mine, 0], qbuf.at[half, mine], keep_sem.at[half, 1])
        copy.start()
        kept[half].append(copy)
        for d in order:
            head = (mine + d) % 4
            copy = remote(
                qkv.at[half, head, pair], kv.at[half, group, mine],
                kv_send.at[half, d - 1], kv_recv.at[half, d - 1], (block_of(head, group), t),
            )
            copy.start()
            kv_copies[half].append(copy)
        for d in order:
            copy = remote(
                qkv.at[half, mine, pair], kv.at[half, group, mine],
                ag_send.at[half, 0, d - 1], ag_recv.at[half, 0, d - 1], (block_of(mine, (group + d) % 4), t),
            )
            copy.start()
            ag_copies[half].append(copy)
        for d in order:
            head = (mine + d) % 4
            copy = remote(
                qkv.at[half, head, 0], qbuf.at[half, mine],
                q_send.at[half, d - 1], q_recv.at[half, d - 1], (block_of(head, group), t),
            )
            copy.start()
            q_copies[half].append(copy)

    def relay(half, i):
        d = order[i]
        kv_copies[half][i].wait_recv()
        slot = (mine + 4 - d) % 4
        for e in order:
            copy = remote(
                kv.at[half, group, slot], kv.at[half, group, slot],
                ag_send.at[half, d, e - 1], ag_recv.at[half, d, e - 1], (block_of(mine, (group + e) % 4), t),
            )
            copy.start()
            ag_copies[half].append(copy)

    def relay_ring(half):
        plus[half][0].wait_recv()
        plus[half][2].start()
        across[half][1].start()
        minus[half][0].wait_recv()
        minus[half][2].start()
        across[half][2].start()

    own_copy.wait()
    for half in range(2):
        if half == 0:
            loads[(0, 0)].wait()
        compute((0, 0), half)
        relay_ring(half)
        if half == 0:
            send_own(1)
            loads[(0, 1)].wait()
        across[half][0].wait_recv()
        compute((0, 1), half)
        if half == 1:
            relay(0, 0)
        plus[half][1].wait_recv()
        across[half][3].start()
        minus[half][1].wait_recv()
        across[half][4].start()
        if half == 0:
            loads[(3, 0)].wait()
        compute((3, 0), half)
        if half == 1:
            relay(0, 1)
        if half == 0:
            loads[(1, 0)].wait()
        compute((1, 0), half)
        if half == 1:
            relay(0, 2)
        across[half][1].wait_recv()
        across[half][3].wait_recv()
        if half == 0:
            loads[(3, 1)].wait()
        compute((3, 1), half)
        across[half][2].wait_recv()
        across[half][4].wait_recv()
        if half == 0:
            loads[(1, 1)].wait()
        compute((1, 1), half)
        plus[half][2].wait_recv()
        across[half][5].start()
        minus[half][2].wait_recv()
        across[half][6].start()
        if half == 0:
            loads[(2, 0)].wait()
        compute((2, 0), half)
        across[half][5].wait_recv()
        across[half][6].wait_recv()
        if half == 0:
            loads[(2, 1)].wait()
        compute((2, 1), half)
        epilogue(half)
        redistribute(half)

    depth_index = iota((HALF, HALF), 0).astype(F32)
    query_index = iota((HALF, HALF), 1).astype(F32)

    def turn(half):
        def one(i, carry):
            keys[half, i // 4, i % 4] = jnp.transpose(kv[half, i // 4, i % 4, 0].astype(F32)).astype(BF16)
            return carry

        lax.fori_loop(0, 16, one, 0)

    def tile(slot, q_half, k_half, back, first, diagonal):
        key_block = block_of(slot, group) - back
        safe = (key_block + 16) % 16
        a = (1 - c) * (safe // 4) + c * (safe % 4)
        g = (1 - c) * (safe % 4) + c * (safe // 4)
        score = jnp.dot(keys[k_half, g, a], qbuf[q_half, slot], preferred_element_type=F32)
        base = (key_block * ROWS + k_half * HALF).astype(F32)
        allowed = depth_index >= lows[q_half, slot] - base
        if diagonal:
            allowed = allowed & (depth_index <= query_index)
        score = jnp.where(allowed, score, LOWEST)
        highest = jnp.max(score, axis=0, keepdims=True)
        if not first:
            previous = peak[q_half, slot]
            highest = jnp.maximum(highest, previous)
        weight = jnp.exp2((score - highest) * FACTOR)
        added = jnp.sum(weight, axis=0, keepdims=True)
        mixed = jnp.dot(kv[k_half, g, a, 1], weight.astype(BF16), preferred_element_type=F32)
        if first:
            total[q_half, slot] = added
            mix[q_half, slot] = mixed
        else:
            fade = jnp.exp2((previous - highest) * FACTOR)
            total[q_half, slot] = total[q_half, slot] * fade + added
            mix[q_half, slot] = mix[q_half, slot] * fade + mixed
        peak[q_half, slot] = highest

    def sweep(q_half, k_half, low, high):
        def one(back, carry):
            for slot in range(4):
                tile(slot, q_half, k_half, back, False, False)
            return carry

        lax.fori_loop(low, high, one, 0)

    def opening(q_half, k_half):
        for slot in range(4):
            tile(slot, q_half, k_half, 0, k_half == 0, q_half == k_half)

    o_copies = [[], []]

    def give_back(half):
        def one(slot, carry):
            done[half, slot] = (mix[half, slot] / total[half, slot]).astype(BF16)
            return carry

        lax.fori_loop(0, 4, one, 0)
        for d in order:
            slot = (mine + d) % 4
            copy = remote(
                done.at[half, slot], heads.at[half, mine],
                o_send.at[half, d - 1], o_recv.at[half, d - 1], (block_of(slot, group), t),
            )
            copy.start()
            o_copies[half].append(copy)
        heads[half, mine] = done[half, mine]

    for copy in kept[0]:
        copy.wait()
    for copy in q_copies[0] + ag_copies[0]:
        copy.wait_recv()
    turn(0)
    opening(0, 0)
    sweep(0, 0, 1, 4)
    relay(1, 0)
    relay(1, 1)
    relay(1, 2)
    sweep(0, 0, 4, 9)
    for copy in kept[1]:
        copy.wait()
    for copy in q_copies[1]:
        copy.wait_recv()
    opening(1, 0)
    sweep(1, 0, 1, 8)

    page_col = jnp.sum(
        jnp.where(iota((32, 32), 0) == iota((32, 32), 1), pages_ref[...].astype(F32), 0.0), axis=1, keepdims=True
    )
    spread_pages = jnp.where(iota((32, ROWS), 0) == iota((32, ROWS), 1) // PAGE, page_col, 0.0)
    shift = (iota((1, ROWS), 1) % PAGE - b * ROWS).astype(F32)
    target = jnp.sum(spread_pages, axis=0, keepdims=True) * PAGE + shift
    chosen = (iota((ROWS, ROWS), 0).astype(F32) == target).astype(F32).astype(BF16)
    for kind in range(2):
        moved = None
        for half in range(2):
            source = jnp.concatenate([qkv[half, h, kind + 1] for h in range(4)], axis=0)
            term = lax.dot_general(
                chosen[:, half * HALF:(half + 1) * HALF], source, (((1,), (1,)), ((), ())),
                preferred_element_type=F32,
            )
            moved = term if moved is None else moved + term
        page_ref[kind] = moved.astype(BF16).reshape(ROWS // PAGE, PAGE, COLS)

    for copy in ag_copies[1]:
        copy.wait_recv()
    turn(1)
    sweep(0, 1, 1, 9)
    give_back(0)

    rs_order = (2, 1, 3, 0)
    ring, across_sums = [{}, {}], [[], []]

    def product(half, key):
        return jnp.dot(x[half], wo[origin(*key)], preferred_element_type=F32)

    def leave(half, i, k, where):
        rows = pl.ds(k * QUARTER, QUARTER)
        n = 2 * i + k
        copy = remote(tx.at[half, i, rows], rx.at[half, i, rows], ring_send.at[half, n], ring_recv.at[half, n], where)
        copy.start()
        ring[half][(i, k)] = copy

    def first_part(half):
        for copy in o_copies[half]:
            copy.wait_recv()
        flat = jnp.concatenate([heads[half, h] for h in range(4)], axis=0).astype(F32)
        x[half] = jnp.transpose(flat).astype(BF16)

        def give(i):
            if half == 0:
                out_loads[(rs_order[i], 1)].wait()
            sib_out[half, i] = product(half, (rs_order[i], 1)).astype(BF16)
            copy = remote(sib_out.at[half, i], sib_in.at[half, i], give_send.at[half, i], give_recv.at[half, i], sibling)
            copy.start()
            across_sums[half].append(copy)

        def own(i):
            if half == 0:
                out_loads[(rs_order[i], 0)].wait()
            value = product(half, (rs_order[i], 0))
            across_sums[half][i].wait_recv()
            return value + sib_in[half, i].astype(F32)

        give(0)
        give(1)
        tx[half, 0] = own(0).astype(BF16)
        leave(half, 0, 0, after)
        leave(half, 0, 1, before)
        give(2)
        value = own(1)
        tx[half, 1, QUARTER:] = value[QUARTER:].astype(BF16)
        leave(half, 1, 1, after)
        hold[half, 0] = value[:QUARTER]
        give(3)
        value = own(2)
        tx[half, 2, :QUARTER] = value[:QUARTER].astype(BF16)
        leave(half, 2, 0, before)
        hold[half, 1] = value[QUARTER:]
        far_hold[half] = own(3)

    def second_part(half):
        ring[half][(0, 0)].wait_recv()
        tx[half, 1, :QUARTER] = (hold[half, 0] + rx[half, 0, :QUARTER].astype(F32)).astype(BF16)
        leave(half, 1, 0, after)
        ring[half][(0, 1)].wait_recv()
        tx[half, 2, QUARTER:] = (hold[half, 1] + rx[half, 0, QUARTER:].astype(F32)).astype(BF16)
        leave(half, 2, 1, before)

    def last_part(half):
        for key in ((1, 1), (2, 0), (1, 0), (2, 1)):
            ring[half][key].wait_recv()
        out_ref[half * HALF:(half + 1) * HALF, :] = (
            far_hold[half] + rx[half, 1].astype(F32) + rx[half, 2].astype(F32)
        ).astype(BF16)

    opening(1, 1)
    sweep(1, 1, 1, 4)
    first_part(0)
    sweep(1, 1, 4, 9)
    give_back(1)
    second_part(0)
    first_part(1)
    last_part(0)
    second_part(1)
    last_part(1)

    for copy in stat_copies:
        copy.wait_send()
    for half in range(2):
        for copy in plus[half] + minus[half] + across[half]:
            copy.wait_send()
        for copy in kv_copies[half] + q_copies[half] + ag_copies[half] + o_copies[half]:
            copy.wait_send()
        for copy in across_sums[half] + list(ring[half].values()):
            copy.wait_send()


VMEM = pl.BlockSpec(memory_space=pltpu.VMEM)
ANY = pl.BlockSpec(memory_space=pl.ANY)
DMA = pltpu.SemaphoreType.DMA


def per_device(hidden_in, ln_gain, w_qkv, w_out, doc_lengths, segment_ids, pair_table, page_table):
    frequency = 10000.0 ** (-(2.0 * (np.arange(ROT) % (ROT // 2))) / ROT)
    frequency = jnp.asarray(np.repeat(frequency[:, None], 128, axis=1), F32)
    scratch = [
        pltpu.VMEM((8, ROWS, SHARD), BF16),
        pltpu.VMEM((3, 8 * SHARD, COLS), BF16),
        pltpu.VMEM((3, HALF, COLS), F32),
        pltpu.VMEM((8, 8, ROWS), F32),
        pltpu.VMEM((2, ROWS, 128), F32),
        pltpu.VMEM((HALF, SHARD), BF16),
        pltpu.VMEM((2, 2, ROT, HALF), F32),
        pltpu.VMEM((2, 4, 3, HD, HALF), BF16),
        pltpu.VMEM((2, 4, HD, HALF), BF16),
        pltpu.VMEM((2, 4, 4, 2, HD, HALF), BF16),
        pltpu.VMEM((2, 4, 4, HALF, HD), BF16),
        pltpu.VMEM((2, 4, 1, HALF), F32),
        pltpu.VMEM((2, 4, 1, HALF), F32),
        pltpu.VMEM((2, 4, 1, HALF), F32),
        pltpu.VMEM((2, 4, HD, HALF), F32),
        pltpu.VMEM((2, 4, HD, HALF), BF16),
        pltpu.VMEM((2, 4, HD, HALF), BF16),
        pltpu.VMEM((8, COLS, SHARD), BF16),
        pltpu.VMEM((2, HALF, COLS), BF16),
        pltpu.VMEM((2, 4, HALF, SHARD), BF16),
        pltpu.VMEM((2, 4, HALF, SHARD), BF16),
        pltpu.VMEM((2, 3, HALF, SHARD), BF16),
        pltpu.VMEM((2, 3, HALF, SHARD), BF16),
        pltpu.VMEM((2, 2, QUARTER, SHARD), F32),
        pltpu.VMEM((2, HALF, SHARD), F32),
        DMA((8,)), DMA((8,)), DMA, DMA((7,)), DMA((7,)), DMA((2, 6)), DMA((2, 6)), DMA((2, 7)), DMA((2, 7)),
        DMA((2, 2)), DMA((2, 3)), DMA((2, 3)), DMA((2, 3)), DMA((2, 3)), DMA((2, 4, 3)), DMA((2, 4, 3)),
        DMA((2, 3)), DMA((2, 3)), DMA((2, 4)), DMA((2, 4)), DMA((2, 6)), DMA((2, 6)),
    ]
    attn_out, pages = pl.pallas_call(
        layer_kernel,
        out_shape=(
            jax.ShapeDtypeStruct((ROWS, SHARD), BF16),
            jax.ShapeDtypeStruct((2, ROWS // PAGE, PAGE, COLS), BF16),
        ),
        in_specs=[VMEM] * 5 + [ANY] * 2,
        out_specs=(VMEM, VMEM),
        scratch_shapes=scratch,
        compiler_params=pltpu.CompilerParams(
            collective_id=0, has_side_effects=True, vmem_limit_bytes=62 * 1024 * 1024
        ),
        name="layer",
    )(
        hidden_in, ln_gain.reshape(8, 1, SHARD), doc_lengths.reshape(1, 64), page_table.reshape(1, 32), frequency,
        jnp.transpose(w_qkv, (1, 0, 2)), w_out,
    )
    return attn_out, pages


def solution(mesh):
    placed = (P("blk", "tp"), P(), P(None, None, "tp"), P("tp", None), P(), P("blk"), P(), P("blk"))
    return jax.shard_map(
        per_device,
        mesh=mesh,
        in_specs=placed,
        out_specs=(P("blk", "tp"), P(None, "blk", None, "tp")),
        check_vma=False,
    )
```

```python
import jax
import jax.numpy as jnp
import numpy as np
from jax import lax
from jax.experimental import pallas as pl
from jax.experimental.pallas import tpu as pltpu
from jax.sharding import PartitionSpec as P

HD = 96
ROT = 24
PAGE = 16
ROWS = 512
HALF = 256
QUARTER = 128
SHARD = 768
COLS = 384
EPSILON = 1e-05
FACTOR = 1.4426950408889634 * HD ** (-0.5)
LOWEST = -1e30
MESH = pl.DeviceIdType.MESH
F32, BF16 = jnp.float32, jnp.bfloat16


def remote(src, dst, send, recv, where):
    return pltpu.make_async_remote_copy(
        src_ref=src, dst_ref=dst, send_sem=send, recv_sem=recv, device_id=where, device_id_type=MESH
    )


def iota(shape, axis):
    return lax.broadcasted_iota(jnp.int32, shape, axis)


def layer_kernel(
    hid_ref, gain_ref, lens_ref, pages_ref, freq_ref, wqkv_ref, wout_ref,
    out_ref, page_ref,
    gathered, wbuf, acc, stats, columns, normed, table, qkv, qbuf, kv, keys, lows,
    scores, peak, total, mix, done, heads, wo, x, sib_in, rx, hold, far_hold,
    w_sem, wo_sem, own_sem, stat_send, stat_recv, ici_send, ici_recv, sib_send, sib_recv,
    keep_sem, kv_send, kv_recv, q_send, q_recv, ag_send, ag_recv, o_send, o_recv,
    give_send, give_recv, ring_send, ring_recv,
):
    b = lax.axis_index("blk")
    t = lax.axis_index("tp")
    z, c = t // 2, t % 2
    y, xx = b // 4, b % 4
    sibling = (b, z * 2 + 1 - c)
    after = (b, ((z + 1) % 4) * 2 + c)
    before = (b, ((z + 3) % 4) * 2 + c)
    mine = (1 - c) * y + c * xx
    group = (1 - c) * xx + c * y
    order = (1, 3, 2)

    def block_of(a, g):
        return (1 - c) * (a * 4 + g) + c * (g * 4 + a)

    def origin(dz, k):
        return ((z + dz) % 4) * 2 + (c + k) % 2

    shard_order = [(0, 0), (0, 1), (3, 0), (1, 0), (3, 1), (1, 1), (2, 0), (2, 1)]
    loads = {}
    for i, key in enumerate(shard_order):
        rows = pl.ds(pl.multiple_of(origin(*key) * SHARD, SHARD), SHARD)
        loads[key] = pltpu.make_async_copy(wqkv_ref.at[:, rows, :], wbuf.at[:, rows, :], w_sem.at[i])
        loads[key].start()
    own_copy = pltpu.make_async_copy(hid_ref, gathered.at[t], own_sem)
    own_copy.start()
    out_loads = {}
    for i, key in enumerate([(2, 1), (2, 0), (1, 1), (1, 0), (3, 1), (3, 0), (0, 1), (0, 0)]):
        who = origin(*key)
        span = pl.ds(pl.multiple_of(who * SHARD, SHARD), SHARD)
        out_loads[key] = pltpu.make_async_copy(wout_ref.at[:, span], wo.at[who], wo_sem.at[i])
        out_loads[key].start()

    barrier = pltpu.get_barrier_semaphore()
    for d in range(1, 8):
        pl.semaphore_signal(barrier, inc=1, device_id=(b, (t + d) % 8), device_id_type=MESH)
    for d in range(1, 4):
        for where in (block_of((mine + d) % 4, group), block_of(mine, (group + d) % 4)):
            pl.semaphore_signal(barrier, inc=1, device_id=(where, t), device_id_type=MESH)

    value = hid_ref[...].astype(F32)
    mean = jnp.sum(value, axis=1, keepdims=True) * (1.0 / SHARD)
    centred = value - mean
    spread = jnp.sum(centred * centred, axis=1, keepdims=True)
    stats[t] = jnp.transpose(jnp.where(iota((ROWS, 128), 1) == 0, mean, spread))[:8]
    pl.semaphore_wait(barrier, 13)

    stat_copies = []
    for d in range(1, 8):
        copy = remote(stats.at[t], stats.at[t], stat_send.at[d - 1], stat_recv.at[d - 1], (b, (t + d) % 8))
        copy.start()
        stat_copies.append(copy)

    def part(half, k):
        return pl.ds(half * HALF + k * QUARTER, QUARTER)

    plus, minus, across = [], [], []
    for half in range(2):
        q0, q1 = part(half, 0), part(half, 1)
        both = pl.ds(half * HALF, HALF)
        left, right, far = origin(3, 0), origin(1, 0), origin(2, 0)

        def ici(i, who, rows, src, where):
            return remote(src.at[rows], gathered.at[who, rows], ici_send.at[half, i], ici_recv.at[half, i], where)

        plus.append([
            ici(0, t, q0, hid_ref, after), ici(1, t, q1, hid_ref, after), ici(2, left, q0, gathered.at[left], after),
        ])
        minus.append([
            ici(3, t, q1, hid_ref, before), ici(4, t, q0, hid_ref, before), ici(5, right, q1, gathered.at[right], before),
        ])
        moved = [(t, both), (left, q0), (right, q1), (left, q1), (right, q0), (far, q0), (far, q1)]
        across.append([
            remote(
                (hid_ref if i == 0 else gathered.at[who]).at[rows], gathered.at[who, rows],
                sib_send.at[half, i], sib_recv.at[half, i], sibling,
            )
            for i, (who, rows) in enumerate(moved)
        ])

    def send_own(half):
        plus[half][0].start()
        minus[half][0].start()
        across[half][0].start()
        plus[half][1].start()
        minus[half][1].start()

    send_own(0)

    lens = lens_ref[...].astype(F32)
    earlier = iota((64, 64), 1) < iota((64, 64), 0)
    starts = jnp.sum(jnp.where(earlier, lens, 0.0), axis=1, keepdims=True)

    def lowest(block, half):
        token = (block * ROWS + half * HALF + iota((1, HALF), 1)).astype(F32)
        return token, jnp.max(jnp.where(starts <= token, starts, 0.0), axis=0, keepdims=True)

    for half in range(2):
        token, low = lowest(b, half)
        angle = freq_ref[:, 0:1] * (token - low)
        table[half, 0] = jnp.cos(angle)
        table[half, 1] = jnp.where(iota((ROT, HALF), 0) < ROT // 2, -1.0, 1.0) * jnp.sin(angle)
        for slot in range(4):
            lows[half, slot] = lowest(block_of(slot, group), half)[1]

    for copy in stat_copies:
        copy.wait_recv()
    means = stats[:, 0, :]
    whole_mean = jnp.sum(means, axis=0, keepdims=True) * 0.125
    off = means - whole_mean
    squares = jnp.sum(stats[:, 1, :], axis=0, keepdims=True) + SHARD * jnp.sum(off * off, axis=0, keepdims=True)
    inverse = lax.rsqrt(squares * (1.0 / (8 * SHARD)) + EPSILON)
    columns[0] = jnp.transpose(jnp.broadcast_to(whole_mean, (128, ROWS)))
    columns[1] = jnp.transpose(jnp.broadcast_to(inverse, (128, ROWS)))

    def compute(key, half):
        who = origin(*key)

        def normalise(i, carry):
            rows = pl.ds(pl.multiple_of(half * HALF + i * 64, 64), 64)
            here = pl.ds(pl.multiple_of(i * 64, 64), 64)
            centre, scale = columns[0, rows, :], columns[1, rows, :]
            for j in range(SHARD // 128):
                span = slice(128 * j, 128 * j + 128)
                normed[here, span] = (
                    (gathered[who, rows, span].astype(F32) - centre) * scale * gain_ref[who, :, span]
                ).astype(BF16)
            return carry

        lax.fori_loop(0, HALF // 64, normalise, 0)
        depth = pl.ds(pl.multiple_of(who * SHARD, SHARD), SHARD)
        fresh = key == (0, 0)

        def multiply(kind, carry):
            product = jnp.dot(normed[...], wbuf[kind, depth, :], preferred_element_type=F32)
            if fresh:
                acc[kind] = product
            else:
                acc[kind] += product
            return carry

        lax.fori_loop(0, 3, multiply, 0)

    def epilogue(half):
        cosine, sine = table[half, 0], table[half, 1]
        for kind in range(3):
            turned = jnp.transpose(acc[kind])
            for h in range(COLS // HD):
                piece = turned[h * HD:(h + 1) * HD]
                if kind < 2:
                    top = piece[:ROT]
                    swapped = jnp.concatenate([top[ROT // 2:], top[:ROT // 2]], axis=0)
                    piece = jnp.concatenate([top * cosine + swapped * sine, piece[ROT:]], axis=0)
                qkv[half, h, kind] = piece.astype(BF16)

    pair = pl.ds(1, 2)
    kept, kv_copies, q_copies, ag_copies = [[], []], [[], []], [[], []], [[], []]

    def redistribute(half):
        copy = pltpu.make_async_copy(qkv.at[half, mine, pair], kv.at[half, group, mine], keep_sem.at[half, 0])
        copy.start()
        kept[half].append(copy)
        copy = pltpu.make_async_copy(qkv.at[half, mine, 0], qbuf.at[half, mine], keep_sem.at[half, 1])
        copy.start()
        kept[half].append(copy)
        for d in order:
            head = (mine + d) % 4
            copy = remote(
                qkv.at[half, head, pair], kv.at[half, group, mine],
                kv_send.at[half, d - 1], kv_recv.at[half, d - 1], (block_of(head, group), t),
            )
            copy.start()
            kv_copies[half].append(copy)
        for d in order:
            copy = remote(
                qkv.at[half, mine, pair], kv.at[half, group, mine],
                ag_send.at[half, 0, d - 1], ag_recv.at[half, 0, d - 1], (block_of(mine, (group + d) % 4), t),
            )
            copy.start()
            ag_copies[half].append(copy)
        for d in order:
            head = (mine + d) % 4
            copy = remote(
                qkv.at[half, head, 0], qbuf.at[half, mine],
                q_send.at[half, d - 1], q_recv.at[half, d - 1], (block_of(head, group), t),
            )
            copy.start()
            q_copies[half].append(copy)

    def relay(half, i):
        d = order[i]
        kv_copies[half][i].wait_recv()
        slot = (mine + 4 - d) % 4
        for e in order:
            copy = remote(
                kv.at[half, group, slot], kv.at[half, group, slot],
                ag_send.at[half, d, e - 1], ag_recv.at[half, d, e - 1], (block_of(mine, (group + e) % 4), t),
            )
            copy.start()
            ag_copies[half].append(copy)

    def relay_ring(half):
        plus[half][0].wait_recv()
        plus[half][2].start()
        across[half][1].start()
        minus[half][0].wait_recv()
        minus[half][2].start()
        across[half][2].start()

    own_copy.wait()
    for half in range(2):
        if half == 0:
            loads[(0, 0)].wait()
        compute((0, 0), half)
        relay_ring(half)
        if half == 0:
            send_own(1)
            loads[(0, 1)].wait()
        across[half][0].wait_recv()
        compute((0, 1), half)
        if half == 1:
            relay(0, 0)
        plus[half][1].wait_recv()
        across[half][3].start()
        minus[half][1].wait_recv()
        across[half][4].start()
        if half == 0:
            loads[(3, 0)].wait()
        compute((3, 0), half)
        if half == 1:
            relay(0, 1)
        if half == 0:
            loads[(1, 0)].wait()
        compute((1, 0), half)
        if half == 1:
            relay(0, 2)
        across[half][1].wait_recv()
        across[half][3].wait_recv()
        if half == 0:
            loads[(3, 1)].wait()
        compute((3, 1), half)
        across[half][2].wait_recv()
        across[half][4].wait_recv()
        if half == 0:
            loads[(1, 1)].wait()
        compute((1, 1), half)
        plus[half][2].wait_recv()
        across[half][5].start()
        minus[half][2].wait_recv()
        across[half][6].start()
        if half == 0:
            loads[(2, 0)].wait()
        compute((2, 0), half)
        across[half][5].wait_recv()
        across[half][6].wait_recv()
        if half == 0:
            loads[(2, 1)].wait()
        compute((2, 1), half)
        epilogue(half)
        redistribute(half)

    depth_index = iota((HALF, HALF), 0).astype(F32)
    query_index = iota((HALF, HALF), 1).astype(F32)

    def turn(half):
        def one(i, carry):
            keys[half, i // 4, i % 4] = jnp.transpose(kv[half, i // 4, i % 4, 0].astype(F32)).astype(BF16)
            return carry

        lax.fori_loop(0, 16, one, 0)

    def unit(slot, q_half, k_half, backs, first):
        query_block = block_of(slot, group)
        low, query = lows[q_half, slot], qbuf[q_half, slot]

        def place(back):
            key_block = query_block - back
            safe = (key_block + 16) % 16
            return key_block, (1 - c) * (safe // 4) + c * (safe % 4), (1 - c) * (safe % 4) + c * (safe // 4)

        rough = None
        for i, back in enumerate(backs):
            key_block, a, g = place(back)
            score = jnp.dot(keys[k_half, g, a], query, preferred_element_type=F32)
            allowed = depth_index >= low - (key_block * ROWS + k_half * HALF).astype(F32)
            if back == 0 and q_half == k_half:
                allowed = allowed & (depth_index <= query_index)
            score = jnp.where(allowed, score, LOWEST)
            scores[i] = score
            tallest = jnp.max(score.reshape(HALF // 8, 8, HALF), axis=0)
            rough = tallest if rough is None else jnp.maximum(rough, tallest)
        highest = jnp.max(rough, axis=0, keepdims=True)
        if not first:
            previous = peak[q_half, slot]
            highest = jnp.maximum(highest, previous)
            fade = jnp.exp2((previous - highest) * FACTOR)
        sums, mixed = None, None
        for i, back in enumerate(backs):
            _, a, g = place(back)
            weight = jnp.exp2((scores[i] - highest) * FACTOR)
            added = jnp.sum(weight.reshape(HALF // 8, 8, HALF), axis=0)
            term = jnp.dot(kv[k_half, g, a, 1], weight.astype(BF16), preferred_element_type=F32)
            sums = added if sums is None else sums + added
            mixed = term if mixed is None else mixed + term
        added = jnp.sum(sums, axis=0, keepdims=True)
        if first:
            total[q_half, slot] = added
            mix[q_half, slot] = mixed
        else:
            total[q_half, slot] = total[q_half, slot] * fade + added
            mix[q_half, slot] = mix[q_half, slot] * fade + mixed
        peak[q_half, slot] = highest

    def sweep(q_half, k_half, low_slot=0, high_slot=4):
        newest = 0 if k_half <= q_half else 1
        oldest = 9 if k_half >= q_half else 8
        backs = list(range(newest, oldest))

        def one(slot, carry):
            unit(slot, q_half, k_half, backs, k_half == 0)
            return carry

        lax.fori_loop(low_slot, high_slot, one, 0)

    o_copies = [[], []]

    def give_back(half):
        def one(slot, carry):
            done[half, slot] = (mix[half, slot] / total[half, slot]).astype(BF16)
            return carry

        lax.fori_loop(0, 4, one, 0)
        for d in order:
            slot = (mine + d) % 4
            copy = remote(
                done.at[half, slot], heads.at[half, mine],
                o_send.at[half, d - 1], o_recv.at[half, d - 1], (block_of(slot, group), t),
            )
            copy.start()
            o_copies[half].append(copy)
        heads[half, mine] = done[half, mine]

    for copy in kept[0]:
        copy.wait()
    for copy in q_copies[0] + ag_copies[0]:
        copy.wait_recv()
    turn(0)
    sweep(0, 0, 0, 2)
    relay(1, 0)
    relay(1, 1)
    relay(1, 2)
    sweep(0, 0, 2, 4)
    for copy in kept[1]:
        copy.wait()
    for copy in q_copies[1]:
        copy.wait_recv()
    sweep(1, 0)

    page_col = jnp.sum(
        jnp.where(iota((32, 32), 0) == iota((32, 32), 1), pages_ref[...].astype(F32), 0.0), axis=1, keepdims=True
    )
    spread_pages = jnp.where(iota((32, ROWS), 0) == iota((32, ROWS), 1) // PAGE, page_col, 0.0)
    shift = (iota((1, ROWS), 1) % PAGE - b * ROWS).astype(F32)
    target = jnp.sum(spread_pages, axis=0, keepdims=True) * PAGE + shift
    chosen = (iota((ROWS, ROWS), 0).astype(F32) == target).astype(F32).astype(BF16)
    for kind in range(2):
        moved = None
        for half in range(2):
            source = jnp.concatenate([qkv[half, h, kind + 1] for h in range(4)], axis=0)
            term = lax.dot_general(
                chosen[:, half * HALF:(half + 1) * HALF], source, (((1,), (1,)), ((), ())),
                preferred_element_type=F32,
            )
            moved = term if moved is None else moved + term
        page_ref[kind] = moved.astype(BF16).reshape(ROWS // PAGE, PAGE, COLS)

    for copy in ag_copies[1]:
        copy.wait_recv()
    turn(1)
    sweep(0, 1)
    give_back(0)

    rs_order = (2, 1, 3, 0)
    ring, across_sums = [{}, {}], [[], []]

    def product(half, key):
        return jnp.dot(x[half], wo[origin(*key)], preferred_element_type=F32)

    def tx(half, i, k):
        return gathered.at[4 + i, part(half, k)]

    def leave(half, i, k, where):
        rows = pl.ds(k * QUARTER, QUARTER)
        n = 2 * i + k
        copy = remote(tx(half, i, k), rx.at[half, i, rows], ring_send.at[half, n], ring_recv.at[half, n], where)
        copy.start()
        ring[half][(i, k)] = copy

    def first_part(half):
        for copy in o_copies[half]:
            copy.wait_recv()
        flat = jnp.concatenate([heads[half, h] for h in range(4)], axis=0).astype(F32)
        x[half] = jnp.transpose(flat).astype(BF16)

        def give(i):
            if half == 0:
                out_loads[(rs_order[i], 1)].wait()
            gathered[i, pl.ds(half * HALF, HALF), :] = product(half, (rs_order[i], 1)).astype(BF16)
            copy = remote(gathered.at[i, pl.ds(half * HALF, HALF)], sib_in.at[half, i], give_send.at[half, i], give_recv.at[half, i], sibling)
            copy.start()
            across_sums[half].append(copy)

        def own(i):
            if half == 0:
                out_loads[(rs_order[i], 0)].wait()
            value = product(half, (rs_order[i], 0))
            across_sums[half][i].wait_recv()
            return value + sib_in[half, i].astype(F32)

        give(0)
        give(1)
        gathered[4, pl.ds(half * HALF, HALF), :] = own(0).astype(BF16)
        leave(half, 0, 0, after)
        leave(half, 0, 1, before)
        give(2)
        value = own(1)
        tx(half, 1, 1)[...] = value[QUARTER:].astype(BF16)
        leave(half, 1, 1, after)
        hold[half, 0] = value[:QUARTER]
        give(3)
        value = own(2)
        tx(half, 2, 0)[...] = value[:QUARTER].astype(BF16)
        leave(half, 2, 0, before)
        hold[half, 1] = value[QUARTER:]
        far_hold[half] = own(3)

    def second_part(half):
        ring[half][(0, 0)].wait_recv()
        tx(half, 1, 0)[...] = (hold[half, 0] + rx[half, 0, :QUARTER].astype(F32)).astype(BF16)
        leave(half, 1, 0, after)
        ring[half][(0, 1)].wait_recv()
        tx(half, 2, 1)[...] = (hold[half, 1] + rx[half, 0, QUARTER:].astype(F32)).astype(BF16)
        leave(half, 2, 1, before)

    def last_part(half):
        for key in ((1, 1), (2, 0), (1, 0), (2, 1)):
            ring[half][key].wait_recv()
        out_ref[half * HALF:(half + 1) * HALF, :] = (
            far_hold[half] + rx[half, 1].astype(F32) + rx[half, 2].astype(F32)
        ).astype(BF16)

    sweep(1, 1, 0, 2)
    for half in range(2):
        for copy in plus[half] + minus[half] + across[half]:
            copy.wait_send()
    first_part(0)
    sweep(1, 1, 2, 4)
    give_back(1)
    second_part(0)
    first_part(1)
    last_part(0)
    second_part(1)
    last_part(1)

    for copy in stat_copies:
        copy.wait_send()
    for half in range(2):
        for copy in kv_copies[half] + q_copies[half] + ag_copies[half] + o_copies[half]:
            copy.wait_send()
        for copy in across_sums[half] + list(ring[half].values()):
            copy.wait_send()


VMEM = pl.BlockSpec(memory_space=pltpu.VMEM)
ANY = pl.BlockSpec(memory_space=pl.ANY)
DMA = pltpu.SemaphoreType.DMA


def per_device(hidden_in, ln_gain, w_qkv, w_out, doc_lengths, segment_ids, pair_table, page_table):
    frequency = 10000.0 ** (-(2.0 * (np.arange(ROT) % (ROT // 2))) / ROT)
    frequency = jnp.asarray(np.repeat(frequency[:, None], 128, axis=1), F32)
    scratch = [
        pltpu.VMEM((8, ROWS, SHARD), BF16),
        pltpu.VMEM((3, 8 * SHARD, COLS), BF16),
        pltpu.VMEM((3, HALF, COLS), F32),
        pltpu.VMEM((8, 8, ROWS), F32),
        pltpu.VMEM((2, ROWS, 128), F32),
        pltpu.VMEM((HALF, SHARD), BF16),
        pltpu.VMEM((2, 2, ROT, HALF), F32),
        pltpu.VMEM((2, 4, 3, HD, HALF), BF16),
        pltpu.VMEM((2, 4, HD, HALF), BF16),
        pltpu.VMEM((2, 4, 4, 2, HD, HALF), BF16),
        pltpu.VMEM((2, 4, 4, HALF, HD), BF16),
        pltpu.VMEM((2, 4, 1, HALF), F32),
        pltpu.VMEM((9, HALF, HALF), F32),
        pltpu.VMEM((2, 4, 1, HALF), F32),
        pltpu.VMEM((2, 4, 1, HALF), F32),
        pltpu.VMEM((2, 4, HD, HALF), F32),
        pltpu.VMEM((2, 4, HD, HALF), BF16),
        pltpu.VMEM((2, 4, HD, HALF), BF16),
        pltpu.VMEM((8, COLS, SHARD), BF16),
        pltpu.VMEM((2, HALF, COLS), BF16),
        pltpu.VMEM((2, 4, HALF, SHARD), BF16),
        pltpu.VMEM((2, 3, HALF, SHARD), BF16),
        pltpu.VMEM((2, 2, QUARTER, SHARD), F32),
        pltpu.VMEM((2, HALF, SHARD), F32),
        DMA((8,)), DMA((8,)), DMA, DMA((7,)), DMA((7,)), DMA((2, 6)), DMA((2, 6)), DMA((2, 7)), DMA((2, 7)),
        DMA((2, 2)), DMA((2, 3)), DMA((2, 3)), DMA((2, 3)), DMA((2, 3)), DMA((2, 4, 3)), DMA((2, 4, 3)),
        DMA((2, 3)), DMA((2, 3)), DMA((2, 4)), DMA((2, 4)), DMA((2, 6)), DMA((2, 6)),
    ]
    attn_out, pages = pl.pallas_call(
        layer_kernel,
        out_shape=(
            jax.ShapeDtypeStruct((ROWS, SHARD), BF16),
            jax.ShapeDtypeStruct((2, ROWS // PAGE, PAGE, COLS), BF16),
        ),
        in_specs=[VMEM] * 5 + [ANY] * 2,
        out_specs=(VMEM, VMEM),
        scratch_shapes=scratch,
        compiler_params=pltpu.CompilerParams(
            collective_id=0, has_side_effects=True, vmem_limit_bytes=49 * 1024 * 1024
        ),
        name="layer",
    )(
        hidden_in, ln_gain.reshape(8, 1, SHARD), doc_lengths.reshape(1, 64), page_table.reshape(1, 32), frequency,
        jnp.transpose(w_qkv, (1, 0, 2)), w_out,
    )
    return attn_out, pages


def solution(mesh):
    placed = (P("blk", "tp"), P(), P(None, None, "tp"), P("tp", None), P(), P("blk"), P(), P("blk"))
    return jax.shard_map(
        per_device,
        mesh=mesh,
        in_specs=placed,
        out_specs=(P("blk", "tp"), P(None, "blk", None, "tp")),
        check_vma=False,
    )
```

```python
import jax
import jax.numpy as jnp
import numpy as np
from jax import lax
from jax.experimental import pallas as pl
from jax.experimental.pallas import tpu as pltpu
from jax.sharding import PartitionSpec as P

HD = 96
ROT = 24
PAGE = 16
ROWS = 512
HALF = 256
QUARTER = 128
SHARD = 768
COLS = 384
EPSILON = 1e-05
FACTOR = 1.4426950408889634 * HD ** (-0.5)
LOWEST = -1e30
MESH = pl.DeviceIdType.MESH
F32, BF16 = jnp.float32, jnp.bfloat16


def remote(src, dst, send, recv, where):
    return pltpu.make_async_remote_copy(
        src_ref=src, dst_ref=dst, send_sem=send, recv_sem=recv, device_id=where, device_id_type=MESH
    )


def iota(shape, axis):
    return lax.broadcasted_iota(jnp.int32, shape, axis)


def layer_kernel(
    hid_ref, gain_ref, lens_ref, pages_ref, freq_ref, wqkv_ref, wout_ref,
    out_ref, page_ref,
    gathered, wbuf, acc, stats, columns, table, qkv, qbuf, kv, keys, lows,
    scores, peak, total, mix, done, heads, wo, x, sib_in, rx, hold, far_hold,
    w_sem, wo_sem, own_sem, stat_send, stat_recv, ici_send, ici_recv, sib_send, sib_recv,
    keep_sem, kv_send, kv_recv, q_send, q_recv, ag_send, ag_recv, o_send, o_recv,
    give_send, give_recv, ring_send, ring_recv,
):
    b = lax.axis_index("blk")
    t = lax.axis_index("tp")
    z, c = t // 2, t % 2
    y, xx = b // 4, b % 4
    sibling = (b, z * 2 + 1 - c)
    after = (b, ((z + 1) % 4) * 2 + c)
    before = (b, ((z + 3) % 4) * 2 + c)
    mine = (1 - c) * y + c * xx
    group = (1 - c) * xx + c * y
    order = (1, 3, 2)

    def block_of(a, g):
        return (1 - c) * (a * 4 + g) + c * (g * 4 + a)

    def origin(dz, k):
        return ((z + dz) % 4) * 2 + (c + k) % 2

    shard_order = [(0, 0), (0, 1), (3, 0), (1, 0), (3, 1), (1, 1), (2, 0), (2, 1)]
    loads = {}
    for i, key in enumerate(shard_order):
        rows = pl.ds(pl.multiple_of(origin(*key) * SHARD, SHARD), SHARD)
        loads[key] = [
            pltpu.make_async_copy(
                wqkv_ref.at[kind, rows, :], wbuf.at[rows, kind * COLS:(kind + 1) * COLS], w_sem.at[i, kind]
            )
            for kind in range(3)
        ]
        for copy in loads[key]:
            copy.start()
    own_copy = pltpu.make_async_copy(hid_ref, gathered.at[t], own_sem)
    own_copy.start()
    out_loads = {}
    for i, key in enumerate([(2, 1), (2, 0), (1, 1), (1, 0), (3, 1), (3, 0), (0, 1), (0, 0)]):
        who = origin(*key)
        span = pl.ds(pl.multiple_of(who * SHARD, SHARD), SHARD)
        out_loads[key] = pltpu.make_async_copy(wout_ref.at[:, span], wo.at[who], wo_sem.at[i])
        out_loads[key].start()

    barrier = pltpu.get_barrier_semaphore()
    for d in range(1, 8):
        pl.semaphore_signal(barrier, inc=1, device_id=(b, (t + d) % 8), device_id_type=MESH)
    for d in range(1, 4):
        for where in (block_of((mine + d) % 4, group), block_of(mine, (group + d) % 4)):
            pl.semaphore_signal(barrier, inc=1, device_id=(where, t), device_id_type=MESH)

    value = hid_ref[...].astype(F32)
    mean = jnp.sum(value, axis=1, keepdims=True) * (1.0 / SHARD)
    centred = value - mean
    spread = jnp.sum(centred * centred, axis=1, keepdims=True)
    stats[t] = jnp.transpose(jnp.where(iota((ROWS, 128), 1) == 0, mean, spread))[:8]
    pl.semaphore_wait(barrier, 13)

    stat_copies = []
    for d in range(1, 8):
        copy = remote(stats.at[t], stats.at[t], stat_send.at[d - 1], stat_recv.at[d - 1], (b, (t + d) % 8))
        copy.start()
        stat_copies.append(copy)

    def part(half, k):
        return pl.ds(half * HALF + k * QUARTER, QUARTER)

    plus, minus, across = [], [], []
    for half in range(2):
        q0, q1 = part(half, 0), part(half, 1)
        both = pl.ds(half * HALF, HALF)
        left, right, far = origin(3, 0), origin(1, 0), origin(2, 0)

        def ici(i, who, rows, src, where):
            return remote(src.at[rows], gathered.at[who, rows], ici_send.at[half, i], ici_recv.at[half, i], where)

        plus.append([
            ici(0, t, q0, hid_ref, after), ici(1, t, q1, hid_ref, after), ici(2, left, q0, gathered.at[left], after),
        ])
        minus.append([
            ici(3, t, q1, hid_ref, before), ici(4, t, q0, hid_ref, before), ici(5, right, q1, gathered.at[right], before),
        ])
        moved = [(t, both), (left, q0), (right, q1), (left, q1), (right, q0), (far, q0), (far, q1)]
        across.append([
            remote(
                (hid_ref if i == 0 else gathered.at[who]).at[rows], gathered.at[who, rows],
                sib_send.at[half, i], sib_recv.at[half, i], sibling,
            )
            for i, (who, rows) in enumerate(moved)
        ])

    def send_own(half):
        plus[half][0].start()
        minus[half][0].start()
        across[half][0].start()
        plus[half][1].start()
        minus[half][1].start()

    send_own(0)

    lens = lens_ref[...].astype(F32)
    earlier = iota((64, 64), 1) < iota((64, 64), 0)
    starts = jnp.sum(jnp.where(earlier, lens, 0.0), axis=1, keepdims=True)

    def lowest(block, half):
        token = (block * ROWS + half * HALF + iota((1, HALF), 1)).astype(F32)
        return token, jnp.max(jnp.where(starts <= token, starts, 0.0), axis=0, keepdims=True)

    for half in range(2):
        token, low = lowest(b, half)
        angle = freq_ref[:, 0:1] * (token - low)
        table[half, 0] = jnp.cos(angle)
        table[half, 1] = jnp.where(iota((ROT, HALF), 0) < ROT // 2, -1.0, 1.0) * jnp.sin(angle)
        for slot in range(4):
            lows[half, slot] = lowest(block_of(slot, group), half)[1]

    for copy in stat_copies:
        copy.wait_recv()
    means = stats[:, 0, :]
    whole_mean = jnp.sum(means, axis=0, keepdims=True) * 0.125
    off = means - whole_mean
    squares = jnp.sum(stats[:, 1, :], axis=0, keepdims=True) + SHARD * jnp.sum(off * off, axis=0, keepdims=True)
    inverse = lax.rsqrt(squares * (1.0 / (8 * SHARD)) + EPSILON)
    columns[0] = jnp.transpose(jnp.broadcast_to(whole_mean, (128, ROWS)))
    columns[1] = jnp.transpose(jnp.broadcast_to(inverse, (128, ROWS)))

    def compute(key, half):
        who = origin(*key)
        rows = slice(half * HALF, (half + 1) * HALF)
        product = None
        for k in range(SHARD // HALF):
            tiles = []
            for j in range(2 * k, 2 * k + 2):
                span = slice(128 * j, 128 * j + 128)
                tiles.append((
                    (gathered[who, rows, span].astype(F32) - columns[0, rows, :])
                    * columns[1, rows, :] * gain_ref[who, :, span]
                ).astype(BF16))
            depth = pl.ds(pl.multiple_of(who * SHARD + k * HALF, HALF), HALF)
            term = jnp.dot(jnp.concatenate(tiles, axis=1), wbuf[depth, :], preferred_element_type=F32)
            product = term if product is None else product + term
        if key == (0, 0):
            acc[...] = product
        else:
            acc[...] += product

    def epilogue(half):
        cosine, sine = table[half, 0], table[half, 1]
        for kind in range(3):
            turned = jnp.transpose(acc[:, kind * COLS:(kind + 1) * COLS])
            for h in range(COLS // HD):
                piece = turned[h * HD:(h + 1) * HD]
                if kind < 2:
                    top = piece[:ROT]
                    swapped = jnp.concatenate([top[ROT // 2:], top[:ROT // 2]], axis=0)
                    piece = jnp.concatenate([top * cosine + swapped * sine, piece[ROT:]], axis=0)
                qkv[half, h, kind] = piece.astype(BF16)

    pair = pl.ds(1, 2)
    kept, kv_copies, q_copies, ag_copies = [[], []], [[], []], [[], []], [[], []]

    def redistribute(half):
        copy = pltpu.make_async_copy(qkv.at[half, mine, pair], kv.at[half, group, mine], keep_sem.at[half, 0])
        copy.start()
        kept[half].append(copy)
        copy = pltpu.make_async_copy(qkv.at[half, mine, 0], qbuf.at[half, mine], keep_sem.at[half, 1])
        copy.start()
        kept[half].append(copy)
        for d in order:
            head = (mine + d) % 4
            copy = remote(
                qkv.at[half, head, pair], kv.at[half, group, mine],
                kv_send.at[half, d - 1], kv_recv.at[half, d - 1], (block_of(head, group), t),
            )
            copy.start()
            kv_copies[half].append(copy)
        for d in order:
            copy = remote(
                qkv.at[half, mine, pair], kv.at[half, group, mine],
                ag_send.at[half, 0, d - 1], ag_recv.at[half, 0, d - 1], (block_of(mine, (group + d) % 4), t),
            )
            copy.start()
            ag_copies[half].append(copy)
        for d in order:
            head = (mine + d) % 4
            copy = remote(
                qkv.at[half, head, 0], qbuf.at[half, mine],
                q_send.at[half, d - 1], q_recv.at[half, d - 1], (block_of(head, group), t),
            )
            copy.start()
            q_copies[half].append(copy)

    def relay(half, i):
        d = order[i]
        kv_copies[half][i].wait_recv()
        slot = (mine + 4 - d) % 4
        for e in order:
            copy = remote(
                kv.at[half, group, slot], kv.at[half, group, slot],
                ag_send.at[half, d, e - 1], ag_recv.at[half, d, e - 1], (block_of(mine, (group + e) % 4), t),
            )
            copy.start()
            ag_copies[half].append(copy)

    def relay_ring(half):
        plus[half][0].wait_recv()
        plus[half][2].start()
        across[half][1].start()
        minus[half][0].wait_recv()
        minus[half][2].start()
        across[half][2].start()

    def ready(key):
        for copy in loads[key]:
            copy.wait()

    own_copy.wait()
    for half in range(2):
        if half == 0:
            ready((0, 0))
        compute((0, 0), half)
        relay_ring(half)
        if half == 0:
            send_own(1)
            ready((0, 1))
        across[half][0].wait_recv()
        compute((0, 1), half)
        if half == 1:
            relay(0, 0)
        plus[half][1].wait_recv()
        across[half][3].start()
        minus[half][1].wait_recv()
        across[half][4].start()
        if half == 0:
            ready((3, 0))
        compute((3, 0), half)
        if half == 1:
            relay(0, 1)
        if half == 0:
            ready((1, 0))
        compute((1, 0), half)
        if half == 1:
            relay(0, 2)
        across[half][1].wait_recv()
        across[half][3].wait_recv()
        if half == 0:
            ready((3, 1))
        compute((3, 1), half)
        across[half][2].wait_recv()
        across[half][4].wait_recv()
        if half == 0:
            ready((1, 1))
        compute((1, 1), half)
        plus[half][2].wait_recv()
        across[half][5].start()
        minus[half][2].wait_recv()
        across[half][6].start()
        if half == 0:
            ready((2, 0))
        compute((2, 0), half)
        across[half][5].wait_recv()
        across[half][6].wait_recv()
        if half == 0:
            ready((2, 1))
        compute((2, 1), half)
        epilogue(half)
        redistribute(half)

    depth_index = iota((HALF, HALF), 0).astype(F32)
    query_index = iota((HALF, HALF), 1).astype(F32)

    def turn(half):
        def one(i, carry):
            keys[half, i // 4, i % 4] = jnp.transpose(kv[half, i // 4, i % 4, 0].astype(F32)).astype(BF16)
            return carry

        lax.fori_loop(0, 16, one, 0)

    def unit(slot, q_half, k_half, backs, first):
        query_block = block_of(slot, group)
        low, query = lows[q_half, slot], qbuf[q_half, slot]

        def place(back):
            key_block = query_block - back
            safe = (key_block + 16) % 16
            return key_block, (1 - c) * (safe // 4) + c * (safe % 4), (1 - c) * (safe % 4) + c * (safe // 4)

        rough = None
        for i, back in enumerate(backs):
            key_block, a, g = place(back)
            score = jnp.dot(keys[k_half, g, a], query, preferred_element_type=F32)
            allowed = depth_index >= low - (key_block * ROWS + k_half * HALF).astype(F32)
            if back == 0 and q_half == k_half:
                allowed = allowed & (depth_index <= query_index)
            score = jnp.where(allowed, score, LOWEST)
            scores[i] = score
            tallest = jnp.max(score.reshape(HALF // 8, 8, HALF), axis=0)
            rough = tallest if rough is None else jnp.maximum(rough, tallest)
        highest = jnp.max(rough, axis=0, keepdims=True)
        if not first:
            previous = peak[q_half, slot]
            highest = jnp.maximum(highest, previous)
            fade = jnp.exp2((previous - highest) * FACTOR)
        sums, mixed = None, None
        for i, back in enumerate(backs):
            _, a, g = place(back)
            weight = jnp.exp2((scores[i] - highest) * FACTOR)
            added = jnp.sum(weight.reshape(HALF // 8, 8, HALF), axis=0)
            term = jnp.dot(kv[k_half, g, a, 1], weight.astype(BF16), preferred_element_type=F32)
            sums = added if sums is None else sums + added
            mixed = term if mixed is None else mixed + term
        added = jnp.sum(sums, axis=0, keepdims=True)
        if first:
            total[q_half, slot] = added
            mix[q_half, slot] = mixed
        else:
            total[q_half, slot] = total[q_half, slot] * fade + added
            mix[q_half, slot] = mix[q_half, slot] * fade + mixed
        peak[q_half, slot] = highest

    def sweep(q_half, k_half, low_slot=0, high_slot=4):
        newest = 0 if k_half <= q_half else 1
        oldest = 9 if k_half >= q_half else 8
        backs = list(range(newest, oldest))

        def one(i, carry):
            slot = (mine + 1 + i) % 4
            unit(slot, q_half, k_half, backs, k_half == 0)
            return carry

        lax.fori_loop(low_slot, high_slot, one, 0)

    o_copies = [[], []]

    def finish(half, slot):
        return (mix[half, slot] / total[half, slot]).astype(BF16)

    def give_back(half):
        def one(i, carry):
            slot = (mine + 1 + i) % 4
            done[half, slot] = finish(half, slot)
            return carry

        lax.fori_loop(0, 3, one, 0)
        for d in order:
            slot = (mine + d) % 4
            copy = remote(
                done.at[half, slot], heads.at[half, mine],
                o_send.at[half, d - 1], o_recv.at[half, d - 1], (block_of(slot, group), t),
            )
            copy.start()
            o_copies[half].append(copy)

    def keep(half):
        heads[half, mine] = finish(half, mine)

    for copy in kept[0]:
        copy.wait()
    for copy in q_copies[0] + ag_copies[0]:
        copy.wait_recv()
    turn(0)
    sweep(0, 0, 0, 2)
    relay(1, 0)
    relay(1, 1)
    relay(1, 2)
    sweep(0, 0, 2, 4)
    for copy in kept[1]:
        copy.wait()
    for copy in q_copies[1]:
        copy.wait_recv()
    sweep(1, 0)

    page_col = jnp.sum(
        jnp.where(iota((32, 32), 0) == iota((32, 32), 1), pages_ref[...].astype(F32), 0.0), axis=1, keepdims=True
    )
    spread_pages = jnp.where(iota((32, ROWS), 0) == iota((32, ROWS), 1) // PAGE, page_col, 0.0)
    shift = (iota((1, ROWS), 1) % PAGE - b * ROWS).astype(F32)
    target = jnp.sum(spread_pages, axis=0, keepdims=True) * PAGE + shift
    chosen = (iota((ROWS, ROWS), 0).astype(F32) == target).astype(F32).astype(BF16)
    for kind in range(2):
        moved = None
        for half in range(2):
            source = jnp.concatenate([qkv[half, h, kind + 1] for h in range(4)], axis=0)
            term = lax.dot_general(
                chosen[:, half * HALF:(half + 1) * HALF], source, (((1,), (1,)), ((), ())),
                preferred_element_type=F32,
            )
            moved = term if moved is None else moved + term
        page_ref[kind] = moved.astype(BF16).reshape(ROWS // PAGE, PAGE, COLS)

    for copy in ag_copies[1]:
        copy.wait_recv()
    turn(1)
    sweep(0, 1, 0, 3)
    give_back(0)
    sweep(0, 1, 3, 4)
    keep(0)

    rs_order = (2, 1, 3, 0)
    ring, across_sums = [{}, {}], [[], []]

    def product(half, key):
        return jnp.dot(x[half], wo[origin(*key)], preferred_element_type=F32)

    def tx(half, i, k):
        return gathered.at[4 + i, part(half, k)]

    def leave(half, i, k, where):
        rows = pl.ds(k * QUARTER, QUARTER)
        n = 2 * i + k
        copy = remote(tx(half, i, k), rx.at[half, i, rows], ring_send.at[half, n], ring_recv.at[half, n], where)
        copy.start()
        ring[half][(i, k)] = copy

    def first_part(half):
        for copy in o_copies[half]:
            copy.wait_recv()
        flat = jnp.concatenate([heads[half, h] for h in range(4)], axis=0).astype(F32)
        x[half] = jnp.transpose(flat).astype(BF16)

        def give(i):
            if half == 0:
                out_loads[(rs_order[i], 1)].wait()
            gathered[i, pl.ds(half * HALF, HALF), :] = product(half, (rs_order[i], 1)).astype(BF16)
            copy = remote(gathered.at[i, pl.ds(half * HALF, HALF)], sib_in.at[half, i], give_send.at[half, i], give_recv.at[half, i], sibling)
            copy.start()
            across_sums[half].append(copy)

        def own(i):
            if half == 0:
                out_loads[(rs_order[i], 0)].wait()
            value = product(half, (rs_order[i], 0))
            across_sums[half][i].wait_recv()
            return value + sib_in[half, i].astype(F32)

        give(0)
        give(1)
        gathered[4, pl.ds(half * HALF, HALF), :] = own(0).astype(BF16)
        leave(half, 0, 0, after)
        leave(half, 0, 1, before)
        give(2)
        value = own(1)
        tx(half, 1, 1)[...] = value[QUARTER:].astype(BF16)
        leave(half, 1, 1, after)
        hold[half, 0] = value[:QUARTER]
        give(3)
        value = own(2)
        tx(half, 2, 0)[...] = value[:QUARTER].astype(BF16)
        leave(half, 2, 0, before)
        hold[half, 1] = value[QUARTER:]
        far_hold[half] = own(3)

    def second_part(half):
        ring[half][(0, 0)].wait_recv()
        tx(half, 1, 0)[...] = (hold[half, 0] + rx[half, 0, :QUARTER].astype(F32)).astype(BF16)
        leave(half, 1, 0, after)
        ring[half][(0, 1)].wait_recv()
        tx(half, 2, 1)[...] = (hold[half, 1] + rx[half, 0, QUARTER:].astype(F32)).astype(BF16)
        leave(half, 2, 1, before)

    def last_part(half):
        for key in ((1, 1), (2, 0), (1, 0), (2, 1)):
            ring[half][key].wait_recv()
        out_ref[half * HALF:(half + 1) * HALF, :] = (
            far_hold[half] + rx[half, 1].astype(F32) + rx[half, 2].astype(F32)
        ).astype(BF16)

    sweep(1, 1, 0, 2)
    for half in range(2):
        for copy in plus[half] + minus[half] + across[half]:
            copy.wait_send()
    first_part(0)
    sweep(1, 1, 2, 3)
    give_back(1)
    second_part(0)
    sweep(1, 1, 3, 4)
    keep(1)
    first_part(1)
    last_part(0)
    second_part(1)
    last_part(1)

    for copy in stat_copies:
        copy.wait_send()
    for half in range(2):
        for copy in kv_copies[half] + q_copies[half] + ag_copies[half] + o_copies[half]:
            copy.wait_send()
        for copy in across_sums[half] + list(ring[half].values()):
            copy.wait_send()


VMEM = pl.BlockSpec(memory_space=pltpu.VMEM)
ANY = pl.BlockSpec(memory_space=pl.ANY)
DMA = pltpu.SemaphoreType.DMA


def per_device(hidden_in, ln_gain, w_qkv, w_out, doc_lengths, segment_ids, pair_table, page_table):
    frequency = 10000.0 ** (-(2.0 * (np.arange(ROT) % (ROT // 2))) / ROT)
    frequency = jnp.asarray(np.repeat(frequency[:, None], 128, axis=1), F32)
    scratch = [
        pltpu.VMEM((8, ROWS, SHARD), BF16),
        pltpu.VMEM((8 * SHARD, 3 * COLS), BF16),
        pltpu.VMEM((HALF, 3 * COLS), F32),
        pltpu.VMEM((8, 8, ROWS), F32),
        pltpu.VMEM((2, ROWS, 128), F32),
        pltpu.VMEM((2, 2, ROT, HALF), F32),
        pltpu.VMEM((2, 4, 3, HD, HALF), BF16),
        pltpu.VMEM((2, 4, HD, HALF), BF16),
        pltpu.VMEM((2, 4, 4, 2, HD, HALF), BF16),
        pltpu.VMEM((2, 4, 4, HALF, HD), BF16),
        pltpu.VMEM((2, 4, 1, HALF), F32),
        pltpu.VMEM((9, HALF, HALF), F32),
        pltpu.VMEM((2, 4, 1, HALF), F32),
        pltpu.VMEM((2, 4, 1, HALF), F32),
        pltpu.VMEM((2, 4, HD, HALF), F32),
        pltpu.VMEM((2, 4, HD, HALF), BF16),
        pltpu.VMEM((2, 4, HD, HALF), BF16),
        pltpu.VMEM((8, COLS, SHARD), BF16),
        pltpu.VMEM((2, HALF, COLS), BF16),
        pltpu.VMEM((2, 4, HALF, SHARD), BF16),
        pltpu.VMEM((2, 3, HALF, SHARD), BF16),
        pltpu.VMEM((2, 2, QUARTER, SHARD), F32),
        pltpu.VMEM((2, HALF, SHARD), F32),
        DMA((8, 3)), DMA((8,)), DMA, DMA((7,)), DMA((7,)), DMA((2, 6)), DMA((2, 6)), DMA((2, 7)), DMA((2, 7)),
        DMA((2, 2)), DMA((2, 3)), DMA((2, 3)), DMA((2, 3)), DMA((2, 3)), DMA((2, 4, 3)), DMA((2, 4, 3)),
        DMA((2, 3)), DMA((2, 3)), DMA((2, 4)), DMA((2, 4)), DMA((2, 6)), DMA((2, 6)),
    ]
    attn_out, pages = pl.pallas_call(
        layer_kernel,
        out_shape=(
            jax.ShapeDtypeStruct((ROWS, SHARD), BF16),
            jax.ShapeDtypeStruct((2, ROWS // PAGE, PAGE, COLS), BF16),
        ),
        in_specs=[VMEM] * 5 + [ANY] * 2,
        out_specs=(VMEM, VMEM),
        scratch_shapes=scratch,
        compiler_params=pltpu.CompilerParams(
            collective_id=0, has_side_effects=True, vmem_limit_bytes=49 * 1024 * 1024
        ),
        name="layer",
    )(
        hidden_in, ln_gain.reshape(8, 1, SHARD), doc_lengths.reshape(1, 64), page_table.reshape(1, 32), frequency,
        jnp.transpose(w_qkv, (1, 0, 2)), w_out,
    )
    return attn_out, pages


def solution(mesh):
    placed = (P("blk", "tp"), P(), P(None, None, "tp"), P("tp", None), P(), P("blk"), P(), P("blk"))
    return jax.shard_map(
        per_device,
        mesh=mesh,
        in_specs=placed,
        out_specs=(P("blk", "tp"), P(None, "blk", None, "tp")),
        check_vma=False,
    )
```

```python
import jax
import jax.numpy as jnp
import numpy as np
from jax import lax
from jax.experimental import pallas as pl
from jax.experimental.pallas import tpu as pltpu
from jax.sharding import PartitionSpec as P

HD = 96
ROT = 24
PAGE = 16
ROWS = 512
HALF = 256
QUARTER = 128
SHARD = 768
COLS = 384
EPSILON = 1e-05
FACTOR = 1.4426950408889634 * HD ** (-0.5)
LOWEST = -1e30
MESH = pl.DeviceIdType.MESH
F32, BF16 = jnp.float32, jnp.bfloat16


def remote(src, dst, send, recv, where):
    return pltpu.make_async_remote_copy(
        src_ref=src, dst_ref=dst, send_sem=send, recv_sem=recv, device_id=where, device_id_type=MESH
    )


def iota(shape, axis):
    return lax.broadcasted_iota(jnp.int32, shape, axis)


def layer_kernel(
    hid_hbm, gain_hbm, lens_hbm, pages_hbm, freq_hbm, wqkv_ref, wout_ref,
    out_ref, page_ref,
    gain_ref, lens_ref, pages_ref, freq_ref, gathered, wbuf, acc, stats, columns, table, qkv, qbuf, kv, keys, lows,
    scores, peak, total, mix, done, heads, wo, x, sib_in, rx, hold, far_hold,
    w_sem, wo_sem, own_sem, small_sem, stat_send, stat_recv, ici_send, ici_recv, sib_send, sib_recv,
    keep_sem, kv_send, kv_recv, q_send, q_recv, ag_send, ag_recv, o_send, o_recv,
    give_send, give_recv, ring_send, ring_recv,
):
    b = lax.axis_index("blk")
    t = lax.axis_index("tp")
    z, c = t // 2, t % 2
    y, xx = b // 4, b % 4
    sibling = (b, z * 2 + 1 - c)
    after = (b, ((z + 1) % 4) * 2 + c)
    before = (b, ((z + 3) % 4) * 2 + c)
    mine = (1 - c) * y + c * xx
    group = (1 - c) * xx + c * y
    order = (1, 3, 2)

    def block_of(a, g):
        return (1 - c) * (a * 4 + g) + c * (g * 4 + a)

    def origin(dz, k):
        return ((z + dz) % 4) * 2 + (c + k) % 2

    barrier = pltpu.get_barrier_semaphore()
    for d in range(1, 8):
        pl.semaphore_signal(barrier, inc=1, device_id=(b, (t + d) % 8), device_id_type=MESH)
    for d in range(1, 4):
        for where in (block_of((mine + d) % 4, group), block_of(mine, (group + d) % 4)):
            pl.semaphore_signal(barrier, inc=1, device_id=(where, t), device_id_type=MESH)

    own_copy = pltpu.make_async_copy(hid_hbm, gathered.at[t], own_sem)
    own_copy.start()
    small = [
        pltpu.make_async_copy(src, dst, small_sem.at[i])
        for i, (src, dst) in enumerate(
            [(lens_hbm, lens_ref), (freq_hbm, freq_ref), (gain_hbm, gain_ref), (pages_hbm, pages_ref)]
        )
    ]
    for copy in small:
        copy.start()

    shard_order = [(0, 0), (0, 1), (3, 0), (1, 0), (3, 1), (1, 1), (2, 0), (2, 1)]
    loads = {}
    for i, key in enumerate(shard_order):
        rows = pl.ds(pl.multiple_of(origin(*key) * SHARD, SHARD), SHARD)
        loads[key] = [
            pltpu.make_async_copy(
                wqkv_ref.at[kind, rows, :], wbuf.at[rows, kind * COLS:(kind + 1) * COLS], w_sem.at[i, kind]
            )
            for kind in range(3)
        ]
        for copy in loads[key]:
            copy.start()
    out_loads = {}
    for i, key in enumerate([(2, 1), (2, 0), (1, 1), (1, 0), (3, 1), (3, 0), (0, 1), (0, 0)]):
        who = origin(*key)
        span = pl.ds(pl.multiple_of(who * SHARD, SHARD), SHARD)
        out_loads[key] = pltpu.make_async_copy(wout_ref.at[:, span], wo.at[who], wo_sem.at[i])
        out_loads[key].start()

    own_copy.wait()
    value = gathered[t].astype(F32)
    mean = jnp.sum(value, axis=1, keepdims=True) * (1.0 / SHARD)
    centred = value - mean
    spread = jnp.sum(centred * centred, axis=1, keepdims=True)
    stats[t] = jnp.transpose(jnp.where(iota((ROWS, 128), 1) == 0, mean, spread))[:8]
    pl.semaphore_wait(barrier, 13)

    stat_copies = []
    for d in range(1, 8):
        copy = remote(stats.at[t], stats.at[t], stat_send.at[d - 1], stat_recv.at[d - 1], (b, (t + d) % 8))
        copy.start()
        stat_copies.append(copy)

    def part(half, k):
        return pl.ds(half * HALF + k * QUARTER, QUARTER)

    plus, minus, across = [], [], []
    for half in range(2):
        q0, q1 = part(half, 0), part(half, 1)
        both = pl.ds(half * HALF, HALF)
        left, right, far = origin(3, 0), origin(1, 0), origin(2, 0)

        def ici(i, who, rows, src, where):
            return remote(src.at[rows], gathered.at[who, rows], ici_send.at[half, i], ici_recv.at[half, i], where)

        plus.append([
            ici(0, t, q0, gathered.at[t], after), ici(1, t, q1, gathered.at[t], after), ici(2, left, q0, gathered.at[left], after),
        ])
        minus.append([
            ici(3, t, q1, gathered.at[t], before), ici(4, t, q0, gathered.at[t], before), ici(5, right, q1, gathered.at[right], before),
        ])
        moved = [(t, both), (left, q0), (right, q1), (left, q1), (right, q0), (far, q0), (far, q1)]
        across.append([
            remote(
                gathered.at[who, rows], gathered.at[who, rows],
                sib_send.at[half, i], sib_recv.at[half, i], sibling,
            )
            for i, (who, rows) in enumerate(moved)
        ])

    def send_own(half):
        plus[half][0].start()
        minus[half][0].start()
        across[half][0].start()
        plus[half][1].start()
        minus[half][1].start()

    send_own(0)

    for copy in small:
        copy.wait()
    lens = lens_ref[...].astype(F32)
    earlier = iota((64, 64), 1) < iota((64, 64), 0)
    starts = jnp.sum(jnp.where(earlier, lens, 0.0), axis=1, keepdims=True)

    def lowest(block, half):
        token = (block * ROWS + half * HALF + iota((1, HALF), 1)).astype(F32)
        return token, jnp.max(jnp.where(starts <= token, starts, 0.0), axis=0, keepdims=True)

    for half in range(2):
        token, low = lowest(b, half)
        angle = freq_ref[:, 0:1] * (token - low)
        table[half, 0] = jnp.cos(angle)
        table[half, 1] = jnp.where(iota((ROT, HALF), 0) < ROT // 2, -1.0, 1.0) * jnp.sin(angle)
        for slot in range(4):
            lows[half, slot] = lowest(block_of(slot, group), half)[1]

    for copy in stat_copies:
        copy.wait_recv()
    means = stats[:, 0, :]
    whole_mean = jnp.sum(means, axis=0, keepdims=True) * 0.125
    off = means - whole_mean
    squares = jnp.sum(stats[:, 1, :], axis=0, keepdims=True) + SHARD * jnp.sum(off * off, axis=0, keepdims=True)
    inverse = lax.rsqrt(squares * (1.0 / (8 * SHARD)) + EPSILON)
    columns[0] = jnp.transpose(jnp.broadcast_to(whole_mean, (128, ROWS)))
    columns[1] = jnp.transpose(jnp.broadcast_to(inverse, (128, ROWS)))

    def compute(key, half):
        who = origin(*key)
        rows = slice(half * HALF, (half + 1) * HALF)
        product = None
        for k in range(SHARD // HALF):
            tiles = []
            for j in range(2 * k, 2 * k + 2):
                span = slice(128 * j, 128 * j + 128)
                tiles.append((
                    (gathered[who, rows, span].astype(F32) - columns[0, rows, :])
                    * columns[1, rows, :] * gain_ref[who, :, span]
                ).astype(BF16))
            depth = pl.ds(pl.multiple_of(who * SHARD + k * HALF, HALF), HALF)
            term = jnp.dot(jnp.concatenate(tiles, axis=1), wbuf[depth, :], preferred_element_type=F32)
            product = term if product is None else product + term
        if key == (0, 0):
            acc[...] = product
        else:
            acc[...] += product

    def epilogue(half):
        cosine, sine = table[half, 0], table[half, 1]
        for kind in range(3):
            turned = jnp.transpose(acc[:, kind * COLS:(kind + 1) * COLS])
            for h in range(COLS // HD):
                piece = turned[h * HD:(h + 1) * HD]
                if kind < 2:
                    top = piece[:ROT]
                    swapped = jnp.concatenate([top[ROT // 2:], top[:ROT // 2]], axis=0)
                    piece = jnp.concatenate([top * cosine + swapped * sine, piece[ROT:]], axis=0)
                qkv[half, h, kind] = piece.astype(BF16)

    pair = pl.ds(1, 2)
    kept, kv_copies, q_copies, ag_copies = [[], []], [[], []], [[], []], [[], []]

    def redistribute(half):
        copy = pltpu.make_async_copy(qkv.at[half, mine, pair], kv.at[half, group, mine], keep_sem.at[half, 0])
        copy.start()
        kept[half].append(copy)
        copy = pltpu.make_async_copy(qkv.at[half, mine, 0], qbuf.at[half, mine], keep_sem.at[half, 1])
        copy.start()
        kept[half].append(copy)
        for d in order:
            head = (mine + d) % 4
            copy = remote(
                qkv.at[half, head, pair], kv.at[half, group, mine],
                kv_send.at[half, d - 1], kv_recv.at[half, d - 1], (block_of(head, group), t),
            )
            copy.start()
            kv_copies[half].append(copy)
        for d in order:
            copy = remote(
                qkv.at[half, mine, pair], kv.at[half, group, mine],
                ag_send.at[half, 0, d - 1], ag_recv.at[half, 0, d - 1], (block_of(mine, (group + d) % 4), t),
            )
            copy.start()
            ag_copies[half].append(copy)
        for d in order:
            head = (mine + d) % 4
            copy = remote(
                qkv.at[half, head, 0], qbuf.at[half, mine],
                q_send.at[half, d - 1], q_recv.at[half, d - 1], (block_of(head, group), t),
            )
            copy.start()
            q_copies[half].append(copy)

    def relay(half, i):
        d = order[i]
        kv_copies[half][i].wait_recv()
        slot = (mine + 4 - d) % 4
        for e in order:
            copy = remote(
                kv.at[half, group, slot], kv.at[half, group, slot],
                ag_send.at[half, d, e - 1], ag_recv.at[half, d, e - 1], (block_of(mine, (group + e) % 4), t),
            )
            copy.start()
            ag_copies[half].append(copy)

    def relay_ring(half):
        plus[half][0].wait_recv()
        plus[half][2].start()
        across[half][1].start()
        minus[half][0].wait_recv()
        minus[half][2].start()
        across[half][2].start()

    def ready(key):
        for copy in loads[key]:
            copy.wait()

    for half in range(2):
        if half == 0:
            ready((0, 0))
        compute((0, 0), half)
        relay_ring(half)
        if half == 0:
            send_own(1)
            ready((0, 1))
        across[half][0].wait_recv()
        compute((0, 1), half)
        if half == 1:
            relay(0, 0)
        plus[half][1].wait_recv()
        across[half][3].start()
        minus[half][1].wait_recv()
        across[half][4].start()
        if half == 0:
            ready((3, 0))
        compute((3, 0), half)
        if half == 1:
            relay(0, 1)
        if half == 0:
            ready((1, 0))
        compute((1, 0), half)
        if half == 1:
            relay(0, 2)
        across[half][1].wait_recv()
        across[half][3].wait_recv()
        if half == 0:
            ready((3, 1))
        compute((3, 1), half)
        across[half][2].wait_recv()
        across[half][4].wait_recv()
        if half == 0:
            ready((1, 1))
        compute((1, 1), half)
        plus[half][2].wait_recv()
        across[half][5].start()
        minus[half][2].wait_recv()
        across[half][6].start()
        if half == 0:
            ready((2, 0))
        compute((2, 0), half)
        across[half][5].wait_recv()
        across[half][6].wait_recv()
        if half == 0:
            ready((2, 1))
        compute((2, 1), half)
        epilogue(half)
        redistribute(half)

    depth_index = iota((HALF, HALF), 0).astype(F32)
    query_index = iota((HALF, HALF), 1).astype(F32)

    def turn(half):
        def one(i, carry):
            keys[half, i // 4, i % 4] = jnp.transpose(kv[half, i // 4, i % 4, 0].astype(F32)).astype(BF16)
            return carry

        lax.fori_loop(0, 16, one, 0)

    def unit(slot, q_half, k_half, backs, first):
        query_block = block_of(slot, group)
        low, query = lows[q_half, slot], qbuf[q_half, slot]

        def place(back):
            key_block = query_block - back
            safe = (key_block + 16) % 16
            return key_block, (1 - c) * (safe // 4) + c * (safe % 4), (1 - c) * (safe % 4) + c * (safe // 4)

        rough = None
        for i, back in enumerate(backs):
            key_block, a, g = place(back)
            score = jnp.dot(keys[k_half, g, a], query, preferred_element_type=F32)
            allowed = depth_index >= low - (key_block * ROWS + k_half * HALF).astype(F32)
            if back == 0 and q_half == k_half:
                allowed = allowed & (depth_index <= query_index)
            score = jnp.where(allowed, score, LOWEST)
            scores[i] = score
            tallest = jnp.max(score.reshape(HALF // 8, 8, HALF), axis=0)
            rough = tallest if rough is None else jnp.maximum(rough, tallest)
        highest = jnp.max(rough, axis=0, keepdims=True)
        if not first:
            previous = peak[q_half, slot]
            highest = jnp.maximum(highest, previous)
            fade = jnp.exp2((previous - highest) * FACTOR)
        sums, mixed = None, None
        for i, back in enumerate(backs):
            _, a, g = place(back)
            weight = jnp.exp2((scores[i] - highest) * FACTOR)
            added = jnp.sum(weight.reshape(HALF // 8, 8, HALF), axis=0)
            term = jnp.dot(kv[k_half, g, a, 1], weight.astype(BF16), preferred_element_type=F32)
            sums = added if sums is None else sums + added
            mixed = term if mixed is None else mixed + term
        added = jnp.sum(sums, axis=0, keepdims=True)
        if first:
            total[q_half, slot] = added
            mix[q_half, slot] = mixed
        else:
            total[q_half, slot] = total[q_half, slot] * fade + added
            mix[q_half, slot] = mix[q_half, slot] * fade + mixed
        peak[q_half, slot] = highest

    def sweep(q_half, k_half, low_slot=0, high_slot=4):
        newest = 0 if k_half <= q_half else 1
        oldest = 9 if k_half >= q_half else 8
        backs = list(range(newest, oldest))

        def one(i, carry):
            slot = (mine + 1 + i) % 4
            unit(slot, q_half, k_half, backs, k_half == 0)
            return carry

        lax.fori_loop(low_slot, high_slot, one, 0)

    o_copies = [[], []]

    def finish(half, slot):
        return (mix[half, slot] / total[half, slot]).astype(BF16)

    def give_back(half):
        def one(i, carry):
            slot = (mine + 1 + i) % 4
            done[half, slot] = finish(half, slot)
            return carry

        lax.fori_loop(0, 3, one, 0)
        for d in order:
            slot = (mine + d) % 4
            copy = remote(
                done.at[half, slot], heads.at[half, mine],
                o_send.at[half, d - 1], o_recv.at[half, d - 1], (block_of(slot, group), t),
            )
            copy.start()
            o_copies[half].append(copy)

    def keep(half):
        heads[half, mine] = finish(half, mine)

    for copy in kept[0]:
        copy.wait()
    for copy in q_copies[0] + ag_copies[0]:
        copy.wait_recv()
    turn(0)
    sweep(0, 0, 0, 2)
    relay(1, 0)
    relay(1, 1)
    relay(1, 2)
    sweep(0, 0, 2, 4)
    for copy in kept[1]:
        copy.wait()
    for copy in q_copies[1]:
        copy.wait_recv()
    sweep(1, 0)

    page_col = jnp.sum(
        jnp.where(iota((32, 32), 0) == iota((32, 32), 1), pages_ref[...].astype(F32), 0.0), axis=1, keepdims=True
    )
    spread_pages = jnp.where(iota((32, ROWS), 0) == iota((32, ROWS), 1) // PAGE, page_col, 0.0)
    shift = (iota((1, ROWS), 1) % PAGE - b * ROWS).astype(F32)
    target = jnp.sum(spread_pages, axis=0, keepdims=True) * PAGE + shift
    chosen = (iota((ROWS, ROWS), 0).astype(F32) == target).astype(F32).astype(BF16)
    for kind in range(2):
        moved = None
        for half in range(2):
            source = jnp.concatenate([qkv[half, h, kind + 1] for h in range(4)], axis=0)
            term = lax.dot_general(
                chosen[:, half * HALF:(half + 1) * HALF], source, (((1,), (1,)), ((), ())),
                preferred_element_type=F32,
            )
            moved = term if moved is None else moved + term
        page_ref[kind] = moved.astype(BF16).reshape(ROWS // PAGE, PAGE, COLS)

    for copy in ag_copies[1]:
        copy.wait_recv()
    turn(1)
    sweep(0, 1, 0, 3)
    give_back(0)
    sweep(0, 1, 3, 4)
    keep(0)

    rs_order = (2, 1, 3, 0)
    ring, across_sums = [{}, {}], [[], []]

    def product(half, key):
        return jnp.dot(x[half], wo[origin(*key)], preferred_element_type=F32)

    def tx(half, i, k):
        return gathered.at[4 + i, part(half, k)]

    def leave(half, i, k, where):
        rows = pl.ds(k * QUARTER, QUARTER)
        n = 2 * i + k
        copy = remote(tx(half, i, k), rx.at[half, i, rows], ring_send.at[half, n], ring_recv.at[half, n], where)
        copy.start()
        ring[half][(i, k)] = copy

    def first_part(half):
        for copy in o_copies[half]:
            copy.wait_recv()
        flat = jnp.concatenate([heads[half, h] for h in range(4)], axis=0).astype(F32)
        x[half] = jnp.transpose(flat).astype(BF16)

        def give(i):
            if half == 0:
                out_loads[(rs_order[i], 1)].wait()
            gathered[i, pl.ds(half * HALF, HALF), :] = product(half, (rs_order[i], 1)).astype(BF16)
            copy = remote(gathered.at[i, pl.ds(half * HALF, HALF)], sib_in.at[half, i], give_send.at[half, i], give_recv.at[half, i], sibling)
            copy.start()
            across_sums[half].append(copy)

        def own(i):
            if half == 0:
                out_loads[(rs_order[i], 0)].wait()
            value = product(half, (rs_order[i], 0))
            across_sums[half][i].wait_recv()
            return value + sib_in[half, i].astype(F32)

        give(0)
        give(1)
        gathered[4, pl.ds(half * HALF, HALF), :] = own(0).astype(BF16)
        leave(half, 0, 0, after)
        leave(half, 0, 1, before)
        give(2)
        value = own(1)
        tx(half, 1, 1)[...] = value[QUARTER:].astype(BF16)
        leave(half, 1, 1, after)
        hold[half, 0] = value[:QUARTER]
        give(3)
        value = own(2)
        tx(half, 2, 0)[...] = value[:QUARTER].astype(BF16)
        leave(half, 2, 0, before)
        hold[half, 1] = value[QUARTER:]
        far_hold[half] = own(3)

    def second_part(half):
        ring[half][(0, 0)].wait_recv()
        tx(half, 1, 0)[...] = (hold[half, 0] + rx[half, 0, :QUARTER].astype(F32)).astype(BF16)
        leave(half, 1, 0, after)
        ring[half][(0, 1)].wait_recv()
        tx(half, 2, 1)[...] = (hold[half, 1] + rx[half, 0, QUARTER:].astype(F32)).astype(BF16)
        leave(half, 2, 1, before)

    def last_part(half):
        for key in ((1, 1), (2, 0), (1, 0), (2, 1)):
            ring[half][key].wait_recv()
        out_ref[half * HALF:(half + 1) * HALF, :] = (
            far_hold[half] + rx[half, 1].astype(F32) + rx[half, 2].astype(F32)
        ).astype(BF16)

    sweep(1, 1, 0, 2)
    for half in range(2):
        for copy in plus[half] + minus[half] + across[half]:
            copy.wait_send()
    first_part(0)
    sweep(1, 1, 2, 3)
    give_back(1)
    second_part(0)
    sweep(1, 1, 3, 4)
    keep(1)
    first_part(1)
    last_part(0)
    second_part(1)
    last_part(1)

    for copy in stat_copies:
        copy.wait_send()
    for half in range(2):
        for copy in kv_copies[half] + q_copies[half] + ag_copies[half] + o_copies[half]:
            copy.wait_send()
        for copy in across_sums[half] + list(ring[half].values()):
            copy.wait_send()


VMEM = pl.BlockSpec(memory_space=pltpu.VMEM)
HBM = pl.BlockSpec(memory_space=pltpu.MemorySpace.HBM)
DMA = pltpu.SemaphoreType.DMA


def per_device(hidden_in, ln_gain, w_qkv, w_out, doc_lengths, segment_ids, pair_table, page_table):
    frequency = 10000.0 ** (-(2.0 * (np.arange(ROT) % (ROT // 2))) / ROT)
    frequency = jnp.asarray(np.repeat(frequency[:, None], 128, axis=1), F32)
    scratch = [
        pltpu.VMEM((8, 1, SHARD), F32),
        pltpu.VMEM((1, 64), jnp.int32),
        pltpu.VMEM((1, 32), jnp.int32),
        pltpu.VMEM((ROT, 128), F32),
        pltpu.VMEM((8, ROWS, SHARD), BF16),
        pltpu.VMEM((8 * SHARD, 3 * COLS), BF16),
        pltpu.VMEM((HALF, 3 * COLS), F32),
        pltpu.VMEM((8, 8, ROWS), F32),
        pltpu.VMEM((2, ROWS, 128), F32),
        pltpu.VMEM((2, 2, ROT, HALF), F32),
        pltpu.VMEM((2, 4, 3, HD, HALF), BF16),
        pltpu.VMEM((2, 4, HD, HALF), BF16),
        pltpu.VMEM((2, 4, 4, 2, HD, HALF), BF16),
        pltpu.VMEM((2, 4, 4, HALF, HD), BF16),
        pltpu.VMEM((2, 4, 1, HALF), F32),
        pltpu.VMEM((9, HALF, HALF), F32),
        pltpu.VMEM((2, 4, 1, HALF), F32),
        pltpu.VMEM((2, 4, 1, HALF), F32),
        pltpu.VMEM((2, 4, HD, HALF), F32),
        pltpu.VMEM((2, 4, HD, HALF), BF16),
        pltpu.VMEM((2, 4, HD, HALF), BF16),
        pltpu.VMEM((8, COLS, SHARD), BF16),
        pltpu.VMEM((2, HALF, COLS), BF16),
        pltpu.VMEM((2, 4, HALF, SHARD), BF16),
        pltpu.VMEM((2, 3, HALF, SHARD), BF16),
        pltpu.VMEM((2, 2, QUARTER, SHARD), F32),
        pltpu.VMEM((2, HALF, SHARD), F32),
        DMA((8, 3)), DMA((8,)), DMA, DMA((4,)), DMA((7,)), DMA((7,)), DMA((2, 6)), DMA((2, 6)), DMA((2, 7)), DMA((2, 7)),
        DMA((2, 2)), DMA((2, 3)), DMA((2, 3)), DMA((2, 3)), DMA((2, 3)), DMA((2, 4, 3)), DMA((2, 4, 3)),
        DMA((2, 3)), DMA((2, 3)), DMA((2, 4)), DMA((2, 4)), DMA((2, 6)), DMA((2, 6)),
    ]
    attn_out, pages = pl.pallas_call(
        layer_kernel,
        out_shape=(
            jax.ShapeDtypeStruct((ROWS, SHARD), BF16),
            jax.ShapeDtypeStruct((2, ROWS // PAGE, PAGE, COLS), BF16),
        ),
        in_specs=[HBM] * 7,
        out_specs=(VMEM, VMEM),
        scratch_shapes=scratch,
        compiler_params=pltpu.CompilerParams(
            collective_id=0, has_side_effects=True, vmem_limit_bytes=49 * 1024 * 1024
        ),
        name="layer",
    )(*[
        pltpu.with_memory_space_constraint(operand, pltpu.MemorySpace.HBM)
        for operand in (
            hidden_in, ln_gain.reshape(8, 1, SHARD), doc_lengths.reshape(1, 64), page_table.reshape(1, 32), frequency,
            jnp.transpose(w_qkv, (1, 0, 2)), w_out,
        )
    ])
    return attn_out, pages


def solution(mesh):
    placed = (P("blk", "tp"), P(), P(None, None, "tp"), P("tp", None), P(), P("blk"), P(), P("blk"))
    return jax.shard_map(
        per_device,
        mesh=mesh,
        in_specs=placed,
        out_specs=(P("blk", "tp"), P(None, "blk", None, "tp")),
        check_vma=False,
    )
```

```python
import jax
import jax.numpy as jnp
import numpy as np
from jax import lax
from jax.experimental import pallas as pl
from jax.experimental.pallas import tpu as pltpu
from jax.sharding import PartitionSpec as P

HD = 96
ROT = 24
PAGE = 16
ROWS = 512
HALF = 256
QUARTER = 128
SHARD = 768
COLS = 384
EPSILON = 1e-05
FACTOR = 1.4426950408889634 * HD ** (-0.5)
LOWEST = -1e30
MESH = pl.DeviceIdType.MESH
F32, BF16 = jnp.float32, jnp.bfloat16


def remote(src, dst, send, recv, where):
    return pltpu.make_async_remote_copy(
        src_ref=src, dst_ref=dst, send_sem=send, recv_sem=recv, device_id=where, device_id_type=MESH
    )


def iota(shape, axis):
    return lax.broadcasted_iota(jnp.int32, shape, axis)


def layer_kernel(
    hid_hbm, gain_hbm, lens_hbm, pages_hbm, freq_hbm, wqkv_ref, wout_ref,
    out_ref, page_ref,
    gain_ref, lens_ref, pages_ref, freq_ref, gathered, wbuf, acc, stats, columns, table, qkv, qbuf, kv, keys, lows,
    scores, peak, total, mix, done, heads, wo, x, sib_in, rx, hold, far_hold,
    w_sem, wo_sem, own_sem, small_sem, stat_send, stat_recv, ici_send, ici_recv, sib_send, sib_recv,
    keep_sem, kv_send, kv_recv, q_send, q_recv, ag_send, ag_recv, o_send, o_recv,
    give_send, give_recv, ring_send, ring_recv,
):
    b = lax.axis_index("blk")
    t = lax.axis_index("tp")
    z, c = t // 2, t % 2
    y, xx = b // 4, b % 4
    sibling = (b, z * 2 + 1 - c)
    after = (b, ((z + 1) % 4) * 2 + c)
    before = (b, ((z + 3) % 4) * 2 + c)
    mine = (1 - c) * y + c * xx
    group = (1 - c) * xx + c * y
    order = (1, 3, 2)

    def block_of(a, g):
        return (1 - c) * (a * 4 + g) + c * (g * 4 + a)

    def origin(dz, k):
        return ((z + dz) % 4) * 2 + (c + k) % 2

    barrier = pltpu.get_barrier_semaphore()
    for d in range(1, 8):
        pl.semaphore_signal(barrier, inc=1, device_id=(b, (t + d) % 8), device_id_type=MESH)
    for d in range(1, 4):
        for where in (block_of((mine + d) % 4, group), block_of(mine, (group + d) % 4)):
            pl.semaphore_signal(barrier, inc=1, device_id=(where, t), device_id_type=MESH)

    own_copy = pltpu.make_async_copy(hid_hbm, gathered.at[t], own_sem)
    own_copy.start()
    small = [
        pltpu.make_async_copy(src, dst, small_sem.at[i])
        for i, (src, dst) in enumerate(
            [(lens_hbm, lens_ref), (freq_hbm, freq_ref), (gain_hbm, gain_ref), (pages_hbm, pages_ref)]
        )
    ]
    for copy in small:
        copy.start()

    shard_order = [(0, 0), (0, 1), (3, 0), (1, 0), (3, 1), (1, 1), (2, 0), (2, 1)]
    loads = {}
    for i, key in enumerate(shard_order):
        rows = pl.ds(pl.multiple_of(origin(*key) * SHARD, SHARD), SHARD)
        loads[key] = [
            pltpu.make_async_copy(
                wqkv_ref.at[kind, rows, :], wbuf.at[rows, kind * COLS:(kind + 1) * COLS], w_sem.at[i, kind]
            )
            for kind in range(3)
        ]
    out_loads = {}
    for i, key in enumerate([(2, 1), (2, 0), (1, 1), (1, 0), (3, 1), (3, 0), (0, 1), (0, 0)]):
        who = origin(*key)
        span = pl.ds(pl.multiple_of(who * SHARD, SHARD), SHARD)
        out_loads[key] = pltpu.make_async_copy(wout_ref.at[:, span], wo.at[who], wo_sem.at[i])

    def fetch(wanted):
        for key in wanted:
            for copy in loads[key]:
                copy.start()

    own_copy.wait()
    for copy in small:
        copy.wait()
    fetch(shard_order[:2])
    value = gathered[t].astype(F32)
    mean = jnp.sum(value, axis=1, keepdims=True) * (1.0 / SHARD)
    centred = value - mean
    spread = jnp.sum(centred * centred, axis=1, keepdims=True)
    stats[t] = jnp.transpose(jnp.where(iota((ROWS, 128), 1) == 0, mean, spread))[:8]
    pl.semaphore_wait(barrier, 13)

    stat_copies = []
    for d in range(1, 8):
        copy = remote(stats.at[t], stats.at[t], stat_send.at[d - 1], stat_recv.at[d - 1], (b, (t + d) % 8))
        copy.start()
        stat_copies.append(copy)

    def part(half, k):
        return pl.ds(half * HALF + k * QUARTER, QUARTER)

    plus, minus, across = [], [], []
    for half in range(2):
        q0, q1 = part(half, 0), part(half, 1)
        both = pl.ds(half * HALF, HALF)
        left, right, far = origin(3, 0), origin(1, 0), origin(2, 0)

        def ici(i, who, rows, src, where):
            return remote(src.at[rows], gathered.at[who, rows], ici_send.at[half, i], ici_recv.at[half, i], where)

        plus.append([
            ici(0, t, q0, gathered.at[t], after), ici(1, t, q1, gathered.at[t], after), ici(2, left, q0, gathered.at[left], after),
        ])
        minus.append([
            ici(3, t, q1, gathered.at[t], before), ici(4, t, q0, gathered.at[t], before), ici(5, right, q1, gathered.at[right], before),
        ])
        moved = [(t, both), (left, q0), (right, q1), (left, q1), (right, q0), (far, q0), (far, q1)]
        across.append([
            remote(
                gathered.at[who, rows], gathered.at[who, rows],
                sib_send.at[half, i], sib_recv.at[half, i], sibling,
            )
            for i, (who, rows) in enumerate(moved)
        ])

    def send_own(half):
        plus[half][0].start()
        minus[half][0].start()
        across[half][0].start()
        plus[half][1].start()
        minus[half][1].start()

    send_own(0)
    fetch(shard_order[2:])

    lens = lens_ref[...].astype(F32)
    earlier = iota((64, 64), 1) < iota((64, 64), 0)
    starts = jnp.sum(jnp.where(earlier, lens, 0.0), axis=1, keepdims=True)

    def lowest(block, half):
        token = (block * ROWS + half * HALF + iota((1, HALF), 1)).astype(F32)
        return token, jnp.max(jnp.where(starts <= token, starts, 0.0), axis=0, keepdims=True)

    for half in range(2):
        token, low = lowest(b, half)
        angle = freq_ref[:, 0:1] * (token - low)
        table[half, 0] = jnp.cos(angle)
        table[half, 1] = jnp.where(iota((ROT, HALF), 0) < ROT // 2, -1.0, 1.0) * jnp.sin(angle)
        for slot in range(4):
            lows[half, slot] = lowest(block_of(slot, group), half)[1]

    for copy in stat_copies:
        copy.wait_recv()
    means = stats[:, 0, :]
    whole_mean = jnp.sum(means, axis=0, keepdims=True) * 0.125
    off = means - whole_mean
    squares = jnp.sum(stats[:, 1, :], axis=0, keepdims=True) + SHARD * jnp.sum(off * off, axis=0, keepdims=True)
    inverse = lax.rsqrt(squares * (1.0 / (8 * SHARD)) + EPSILON)
    columns[0] = jnp.transpose(jnp.broadcast_to(whole_mean, (128, ROWS)))
    columns[1] = jnp.transpose(jnp.broadcast_to(inverse, (128, ROWS)))

    def compute(key, half):
        who = origin(*key)
        rows = slice(half * HALF, (half + 1) * HALF)
        product = None
        for k in range(SHARD // HALF):
            tiles = []
            for j in range(2 * k, 2 * k + 2):
                span = slice(128 * j, 128 * j + 128)
                tiles.append((
                    (gathered[who, rows, span].astype(F32) - columns[0, rows, :])
                    * columns[1, rows, :] * gain_ref[who, :, span]
                ).astype(BF16))
            depth = pl.ds(pl.multiple_of(who * SHARD + k * HALF, HALF), HALF)
            term = jnp.dot(jnp.concatenate(tiles, axis=1), wbuf[depth, :], preferred_element_type=F32)
            product = term if product is None else product + term
        if key == (0, 0):
            acc[...] = product
        else:
            acc[...] += product

    def epilogue(half):
        cosine, sine = table[half, 0], table[half, 1]
        for kind in range(3):
            turned = jnp.transpose(acc[:, kind * COLS:(kind + 1) * COLS])
            for h in range(COLS // HD):
                piece = turned[h * HD:(h + 1) * HD]
                if kind < 2:
                    top = piece[:ROT]
                    swapped = jnp.concatenate([top[ROT // 2:], top[:ROT // 2]], axis=0)
                    piece = jnp.concatenate([top * cosine + swapped * sine, piece[ROT:]], axis=0)
                qkv[half, h, kind] = piece.astype(BF16)

    pair = pl.ds(1, 2)
    kept, kv_copies, q_copies, ag_copies = [[], []], [[], []], [[], []], [[], []]

    def redistribute(half):
        copy = pltpu.make_async_copy(qkv.at[half, mine, pair], kv.at[half, group, mine], keep_sem.at[half, 0])
        copy.start()
        kept[half].append(copy)
        copy = pltpu.make_async_copy(qkv.at[half, mine, 0], qbuf.at[half, mine], keep_sem.at[half, 1])
        copy.start()
        kept[half].append(copy)
        for d in order:
            head = (mine + d) % 4
            copy = remote(
                qkv.at[half, head, pair], kv.at[half, group, mine],
                kv_send.at[half, d - 1], kv_recv.at[half, d - 1], (block_of(head, group), t),
            )
            copy.start()
            kv_copies[half].append(copy)
        for d in order:
            copy = remote(
                qkv.at[half, mine, pair], kv.at[half, group, mine],
                ag_send.at[half, 0, d - 1], ag_recv.at[half, 0, d - 1], (block_of(mine, (group + d) % 4), t),
            )
            copy.start()
            ag_copies[half].append(copy)
        for d in order:
            head = (mine + d) % 4
            copy = remote(
                qkv.at[half, head, 0], qbuf.at[half, mine],
                q_send.at[half, d - 1], q_recv.at[half, d - 1], (block_of(head, group), t),
            )
            copy.start()
            q_copies[half].append(copy)

    def relay(half, i):
        d = order[i]
        kv_copies[half][i].wait_recv()
        slot = (mine + 4 - d) % 4
        for e in order:
            copy = remote(
                kv.at[half, group, slot], kv.at[half, group, slot],
                ag_send.at[half, d, e - 1], ag_recv.at[half, d, e - 1], (block_of(mine, (group + e) % 4), t),
            )
            copy.start()
            ag_copies[half].append(copy)

    def relay_ring(half):
        plus[half][0].wait_recv()
        plus[half][2].start()
        across[half][1].start()
        minus[half][0].wait_recv()
        minus[half][2].start()
        across[half][2].start()

    def ready(key):
        for copy in loads[key]:
            copy.wait()

    for half in range(2):
        if half == 0:
            ready((0, 0))
        compute((0, 0), half)
        relay_ring(half)
        if half == 0:
            send_own(1)
            ready((0, 1))
        else:
            for copy in out_loads.values():
                copy.start()
        across[half][0].wait_recv()
        compute((0, 1), half)
        if half == 1:
            relay(0, 0)
        plus[half][1].wait_recv()
        across[half][3].start()
        minus[half][1].wait_recv()
        across[half][4].start()
        if half == 0:
            ready((3, 0))
        compute((3, 0), half)
        if half == 1:
            relay(0, 1)
        if half == 0:
            ready((1, 0))
        compute((1, 0), half)
        if half == 1:
            relay(0, 2)
        across[half][1].wait_recv()
        across[half][3].wait_recv()
        if half == 0:
            ready((3, 1))
        compute((3, 1), half)
        across[half][2].wait_recv()
        across[half][4].wait_recv()
        if half == 0:
            ready((1, 1))
        compute((1, 1), half)
        plus[half][2].wait_recv()
        across[half][5].start()
        minus[half][2].wait_recv()
        across[half][6].start()
        if half == 0:
            ready((2, 0))
        compute((2, 0), half)
        across[half][5].wait_recv()
        across[half][6].wait_recv()
        if half == 0:
            ready((2, 1))
        compute((2, 1), half)
        epilogue(half)
        redistribute(half)

    depth_index = iota((HALF, HALF), 0).astype(F32)
    query_index = iota((HALF, HALF), 1).astype(F32)

    def turn(half):
        def one(i, carry):
            keys[half, i // 4, i % 4] = jnp.transpose(kv[half, i // 4, i % 4, 0].astype(F32)).astype(BF16)
            return carry

        lax.fori_loop(0, 16, one, 0)

    def unit(slot, q_half, k_half, backs, first):
        query_block = block_of(slot, group)
        low, query = lows[q_half, slot], qbuf[q_half, slot]

        def place(back):
            key_block = query_block - back
            safe = (key_block + 16) % 16
            return key_block, (1 - c) * (safe // 4) + c * (safe % 4), (1 - c) * (safe % 4) + c * (safe // 4)

        rough = None
        for i, back in enumerate(backs):
            key_block, a, g = place(back)
            score = jnp.dot(keys[k_half, g, a], query, preferred_element_type=F32)
            allowed = depth_index >= low - (key_block * ROWS + k_half * HALF).astype(F32)
            if back == 0 and q_half == k_half:
                allowed = allowed & (depth_index <= query_index)
            score = jnp.where(allowed, score, LOWEST)
            scores[i] = score
            tallest = jnp.max(score.reshape(HALF // 8, 8, HALF), axis=0)
            rough = tallest if rough is None else jnp.maximum(rough, tallest)
        highest = jnp.max(rough, axis=0, keepdims=True)
        if not first:
            previous = peak[q_half, slot]
            highest = jnp.maximum(highest, previous)
            fade = jnp.exp2((previous - highest) * FACTOR)
        sums, mixed = None, None
        for i, back in enumerate(backs):
            _, a, g = place(back)
            weight = jnp.exp2((scores[i] - highest) * FACTOR)
            added = jnp.sum(weight.reshape(HALF // 8, 8, HALF), axis=0)
            term = jnp.dot(kv[k_half, g, a, 1], weight.astype(BF16), preferred_element_type=F32)
            sums = added if sums is None else sums + added
            mixed = term if mixed is None else mixed + term
        added = jnp.sum(sums, axis=0, keepdims=True)
        if first:
            total[q_half, slot] = added
            mix[q_half, slot] = mixed
        else:
            total[q_half, slot] = total[q_half, slot] * fade + added
            mix[q_half, slot] = mix[q_half, slot] * fade + mixed
        peak[q_half, slot] = highest

    def sweep(q_half, k_half, low_slot=0, high_slot=4):
        newest = 0 if k_half <= q_half else 1
        oldest = 9 if k_half >= q_half else 8
        backs = list(range(newest, oldest))

        def one(i, carry):
            slot = (mine + 1 + i) % 4
            unit(slot, q_half, k_half, backs, k_half == 0)
            return carry

        lax.fori_loop(low_slot, high_slot, one, 0)

    o_copies = [[], []]

    def finish(half, slot):
        return (mix[half, slot] / total[half, slot]).astype(BF16)

    def give_back(half):
        def one(i, carry):
            slot = (mine + 1 + i) % 4
            done[half, slot] = finish(half, slot)
            return carry

        lax.fori_loop(0, 3, one, 0)
        for d in order:
            slot = (mine + d) % 4
            copy = remote(
                done.at[half, slot], heads.at[half, mine],
                o_send.at[half, d - 1], o_recv.at[half, d - 1], (block_of(slot, group), t),
            )
            copy.start()
            o_copies[half].append(copy)

    def keep(half):
        heads[half, mine] = finish(half, mine)

    for copy in kept[0]:
        copy.wait()
    for copy in q_copies[0] + ag_copies[0]:
        copy.wait_recv()
    turn(0)
    sweep(0, 0, 0, 2)
    relay(1, 0)
    relay(1, 1)
    relay(1, 2)
    sweep(0, 0, 2, 4)
    for copy in kept[1]:
        copy.wait()
    for copy in q_copies[1]:
        copy.wait_recv()
    sweep(1, 0)

    page_col = jnp.sum(
        jnp.where(iota((32, 32), 0) == iota((32, 32), 1), pages_ref[...].astype(F32), 0.0), axis=1, keepdims=True
    )
    spread_pages = jnp.where(iota((32, ROWS), 0) == iota((32, ROWS), 1) // PAGE, page_col, 0.0)
    shift = (iota((1, ROWS), 1) % PAGE - b * ROWS).astype(F32)
    target = jnp.sum(spread_pages, axis=0, keepdims=True) * PAGE + shift
    chosen = (iota((ROWS, ROWS), 0).astype(F32) == target).astype(F32).astype(BF16)
    for kind in range(2):
        moved = None
        for half in range(2):
            source = jnp.concatenate([qkv[half, h, kind + 1] for h in range(4)], axis=0)
            term = lax.dot_general(
                chosen[:, half * HALF:(half + 1) * HALF], source, (((1,), (1,)), ((), ())),
                preferred_element_type=F32,
            )
            moved = term if moved is None else moved + term
        page_ref[kind] = moved.astype(BF16).reshape(ROWS // PAGE, PAGE, COLS)

    for copy in ag_copies[1]:
        copy.wait_recv()
    turn(1)
    sweep(0, 1, 0, 3)
    give_back(0)
    sweep(0, 1, 3, 4)
    keep(0)

    rs_order = (2, 1, 3, 0)
    ring, across_sums = [{}, {}], [[], []]

    def product(half, key):
        return jnp.dot(x[half], wo[origin(*key)], preferred_element_type=F32)

    def tx(half, i, k):
        return gathered.at[4 + i, part(half, k)]

    def leave(half, i, k, where):
        rows = pl.ds(k * QUARTER, QUARTER)
        n = 2 * i + k
        copy = remote(tx(half, i, k), rx.at[half, i, rows], ring_send.at[half, n], ring_recv.at[half, n], where)
        copy.start()
        ring[half][(i, k)] = copy

    def first_part(half):
        for copy in o_copies[half]:
            copy.wait_recv()
        flat = jnp.concatenate([heads[half, h] for h in range(4)], axis=0).astype(F32)
        x[half] = jnp.transpose(flat).astype(BF16)

        def give(i):
            if half == 0:
                out_loads[(rs_order[i], 1)].wait()
            gathered[i, pl.ds(half * HALF, HALF), :] = product(half, (rs_order[i], 1)).astype(BF16)
            copy = remote(gathered.at[i, pl.ds(half * HALF, HALF)], sib_in.at[half, i], give_send.at[half, i], give_recv.at[half, i], sibling)
            copy.start()
            across_sums[half].append(copy)

        def own(i):
            if half == 0:
                out_loads[(rs_order[i], 0)].wait()
            value = product(half, (rs_order[i], 0))
            across_sums[half][i].wait_recv()
            return value + sib_in[half, i].astype(F32)

        give(0)
        give(1)
        gathered[4, pl.ds(half * HALF, HALF), :] = own(0).astype(BF16)
        leave(half, 0, 0, after)
        leave(half, 0, 1, before)
        give(2)
        value = own(1)
        tx(half, 1, 1)[...] = value[QUARTER:].astype(BF16)
        leave(half, 1, 1, after)
        hold[half, 0] = value[:QUARTER]
        give(3)
        value = own(2)
        tx(half, 2, 0)[...] = value[:QUARTER].astype(BF16)
        leave(half, 2, 0, before)
        hold[half, 1] = value[QUARTER:]
        far_hold[half] = own(3)

    def second_part(half):
        ring[half][(0, 0)].wait_recv()
        tx(half, 1, 0)[...] = (hold[half, 0] + rx[half, 0, :QUARTER].astype(F32)).astype(BF16)
        leave(half, 1, 0, after)
        ring[half][(0, 1)].wait_recv()
        tx(half, 2, 1)[...] = (hold[half, 1] + rx[half, 0, QUARTER:].astype(F32)).astype(BF16)
        leave(half, 2, 1, before)

    def last_part(half):
        for key in ((1, 1), (2, 0), (1, 0), (2, 1)):
            ring[half][key].wait_recv()
        out_ref[half * HALF:(half + 1) * HALF, :] = (
            far_hold[half] + rx[half, 1].astype(F32) + rx[half, 2].astype(F32)
        ).astype(BF16)

    sweep(1, 1, 0, 2)
    for half in range(2):
        for copy in plus[half] + minus[half] + across[half]:
            copy.wait_send()
    first_part(0)
    sweep(1, 1, 2, 3)
    give_back(1)
    second_part(0)
    sweep(1, 1, 3, 4)
    keep(1)
    first_part(1)
    last_part(0)
    second_part(1)
    last_part(1)

    for copy in stat_copies:
        copy.wait_send()
    for half in range(2):
        for copy in kv_copies[half] + q_copies[half] + ag_copies[half] + o_copies[half]:
            copy.wait_send()
        for copy in across_sums[half] + list(ring[half].values()):
            copy.wait_send()


VMEM = pl.BlockSpec(memory_space=pltpu.VMEM)
HBM = pl.BlockSpec(memory_space=pltpu.MemorySpace.HBM)
DMA = pltpu.SemaphoreType.DMA


def per_device(hidden_in, ln_gain, w_qkv, w_out, doc_lengths, segment_ids, pair_table, page_table):
    frequency = 10000.0 ** (-(2.0 * (np.arange(ROT) % (ROT // 2))) / ROT)
    frequency = jnp.asarray(np.repeat(frequency[:, None], 128, axis=1), F32)
    scratch = [
        pltpu.VMEM((8, 1, SHARD), F32),
        pltpu.VMEM((1, 64), jnp.int32),
        pltpu.VMEM((1, 32), jnp.int32),
        pltpu.VMEM((ROT, 128), F32),
        pltpu.VMEM((8, ROWS, SHARD), BF16),
        pltpu.VMEM((8 * SHARD, 3 * COLS), BF16),
        pltpu.VMEM((HALF, 3 * COLS), F32),
        pltpu.VMEM((8, 8, ROWS), F32),
        pltpu.VMEM((2, ROWS, 128), F32),
        pltpu.VMEM((2, 2, ROT, HALF), F32),
        pltpu.VMEM((2, 4, 3, HD, HALF), BF16),
        pltpu.VMEM((2, 4, HD, HALF), BF16),
        pltpu.VMEM((2, 4, 4, 2, HD, HALF), BF16),
        pltpu.VMEM((2, 4, 4, HALF, HD), BF16),
        pltpu.VMEM((2, 4, 1, HALF), F32),
        pltpu.VMEM((9, HALF, HALF), F32),
        pltpu.VMEM((2, 4, 1, HALF), F32),
        pltpu.VMEM((2, 4, 1, HALF), F32),
        pltpu.VMEM((2, 4, HD, HALF), F32),
        pltpu.VMEM((2, 4, HD, HALF), BF16),
        pltpu.VMEM((2, 4, HD, HALF), BF16),
        pltpu.VMEM((8, COLS, SHARD), BF16),
        pltpu.VMEM((2, HALF, COLS), BF16),
        pltpu.VMEM((2, 4, HALF, SHARD), BF16),
        pltpu.VMEM((2, 3, HALF, SHARD), BF16),
        pltpu.VMEM((2, 2, QUARTER, SHARD), F32),
        pltpu.VMEM((2, HALF, SHARD), F32),
        DMA((8, 3)), DMA((8,)), DMA, DMA((4,)), DMA((7,)), DMA((7,)), DMA((2, 6)), DMA((2, 6)), DMA((2, 7)), DMA((2, 7)),
        DMA((2, 2)), DMA((2, 3)), DMA((2, 3)), DMA((2, 3)), DMA((2, 3)), DMA((2, 4, 3)), DMA((2, 4, 3)),
        DMA((2, 3)), DMA((2, 3)), DMA((2, 4)), DMA((2, 4)), DMA((2, 6)), DMA((2, 6)),
    ]
    attn_out, pages = pl.pallas_call(
        layer_kernel,
        out_shape=(
            jax.ShapeDtypeStruct((ROWS, SHARD), BF16),
            jax.ShapeDtypeStruct((2, ROWS // PAGE, PAGE, COLS), BF16),
        ),
        in_specs=[HBM] * 7,
        out_specs=(VMEM, VMEM),
        scratch_shapes=scratch,
        compiler_params=pltpu.CompilerParams(
            collective_id=0, has_side_effects=True, vmem_limit_bytes=49 * 1024 * 1024
        ),
        name="layer",
    )(*[
        pltpu.with_memory_space_constraint(operand, pltpu.MemorySpace.HBM)
        for operand in (
            hidden_in, ln_gain.reshape(8, 1, SHARD), doc_lengths.reshape(1, 64), page_table.reshape(1, 32), frequency,
            jnp.transpose(w_qkv, (1, 0, 2)), w_out,
        )
    ])
    return attn_out, pages


def solution(mesh):
    placed = (P("blk", "tp"), P(), P(None, None, "tp"), P("tp", None), P(), P("blk"), P(), P("blk"))
    return jax.shard_map(
        per_device,
        mesh=mesh,
        in_specs=placed,
        out_specs=(P("blk", "tp"), P(None, "blk", None, "tp")),
        check_vma=False,
    )
```

```python
import jax
import jax.numpy as jnp
import numpy as np
from jax import lax
from jax.experimental import pallas as pl
from jax.experimental.pallas import tpu as pltpu
from jax.sharding import PartitionSpec as P

HD = 96
ROT = 24
PAGE = 16
ROWS = 512
HALF = 256
QUARTER = 128
SHARD = 768
COLS = 384
EPSILON = 1e-05
FACTOR = 1.4426950408889634 * HD ** (-0.5)
LOWEST = -1e30
MESH = pl.DeviceIdType.MESH
F32, BF16 = jnp.float32, jnp.bfloat16


def remote(src, dst, send, recv, where):
    return pltpu.make_async_remote_copy(
        src_ref=src, dst_ref=dst, send_sem=send, recv_sem=recv, device_id=where, device_id_type=MESH
    )


def iota(shape, axis):
    return lax.broadcasted_iota(jnp.int32, shape, axis)


def layer_kernel(
    hid_hbm, gain_hbm, lens_hbm, pages_hbm, freq_hbm, wqkv_ref, wout_ref,
    out_ref, page_ref,
    gain_ref, lens_ref, pages_ref, freq_ref, gathered, wbuf, acc, stats, columns, table, qkv, qbuf, kv, keys, lows,
    scores, peak, total, mix, done, heads, wo, x, sib_in, rx, hold, far_hold,
    w_sem, wo_sem, own_sem, small_sem, stat_send, stat_recv, ici_send, ici_recv, sib_send, sib_recv,
    keep_sem, kv_send, kv_recv, q_send, q_recv, ag_send, ag_recv, o_send, o_recv,
    give_send, give_recv, ring_send, ring_recv,
):
    b = lax.axis_index("blk")
    t = lax.axis_index("tp")
    z, c = t // 2, t % 2
    y, xx = b // 4, b % 4
    sibling = (b, z * 2 + 1 - c)
    after = (b, ((z + 1) % 4) * 2 + c)
    before = (b, ((z + 3) % 4) * 2 + c)
    mine = (1 - c) * y + c * xx
    group = (1 - c) * xx + c * y
    order = (1, 3, 2)

    def block_of(a, g):
        return (1 - c) * (a * 4 + g) + c * (g * 4 + a)

    def origin(dz, k):
        return ((z + dz) % 4) * 2 + (c + k) % 2

    barrier = pltpu.get_barrier_semaphore()
    for d in range(1, 8):
        pl.semaphore_signal(barrier, inc=1, device_id=(b, (t + d) % 8), device_id_type=MESH)
    for d in range(1, 4):
        for where in (block_of((mine + d) % 4, group), block_of(mine, (group + d) % 4)):
            pl.semaphore_signal(barrier, inc=1, device_id=(where, t), device_id_type=MESH)

    own_copy = pltpu.make_async_copy(hid_hbm, gathered.at[t], own_sem)
    own_copy.start()
    small = [
        pltpu.make_async_copy(src, dst, small_sem.at[i])
        for i, (src, dst) in enumerate(
            [(lens_hbm, lens_ref), (freq_hbm, freq_ref), (gain_hbm, gain_ref), (pages_hbm, pages_ref)]
        )
    ]
    for copy in small:
        copy.start()

    shard_order = [(0, 0), (0, 1), (3, 0), (1, 0), (3, 1), (1, 1), (2, 0), (2, 1)]
    loads = {}
    for i, key in enumerate(shard_order):
        rows = pl.ds(pl.multiple_of(origin(*key) * SHARD, SHARD), SHARD)
        loads[key] = [
            pltpu.make_async_copy(
                wqkv_ref.at[kind, rows, :], wbuf.at[rows, kind * COLS:(kind + 1) * COLS], w_sem.at[i, kind]
            )
            for kind in range(3)
        ]
    out_loads = {}
    for i, key in enumerate([(2, 1), (2, 0), (1, 1), (1, 0), (3, 1), (3, 0), (0, 1), (0, 0)]):
        who = origin(*key)
        span = pl.ds(pl.multiple_of(who * SHARD, SHARD), SHARD)
        out_loads[key] = pltpu.make_async_copy(wout_ref.at[:, span], wo.at[who], wo_sem.at[i])

    def fetch(wanted):
        for key in wanted:
            for copy in loads[key]:
                copy.start()

    own_copy.wait()
    for copy in small:
        copy.wait()
    fetch(shard_order[:2])
    value = gathered[t].astype(F32)
    mean = jnp.sum(value, axis=1, keepdims=True) * (1.0 / SHARD)
    centred = value - mean
    spread = jnp.sum(centred * centred, axis=1, keepdims=True)
    stats[t] = jnp.transpose(jnp.where(iota((ROWS, 128), 1) == 0, mean, spread))[:8]
    pl.semaphore_wait(barrier, 13)

    stat_copies = []
    for d in range(1, 8):
        copy = remote(stats.at[t], stats.at[t], stat_send.at[d - 1], stat_recv.at[d - 1], (b, (t + d) % 8))
        copy.start()
        stat_copies.append(copy)

    def part(half, k):
        return pl.ds(half * HALF + k * QUARTER, QUARTER)

    plus, minus, across = [], [], []
    for half in range(2):
        q0, q1 = part(half, 0), part(half, 1)
        both = pl.ds(half * HALF, HALF)
        left, right, far = origin(3, 0), origin(1, 0), origin(2, 0)

        def ici(i, who, rows, src, where):
            return remote(src.at[rows], gathered.at[who, rows], ici_send.at[half, i], ici_recv.at[half, i], where)

        plus.append([
            ici(0, t, q0, gathered.at[t], after), ici(1, t, q1, gathered.at[t], after), ici(2, left, q0, gathered.at[left], after),
        ])
        minus.append([
            ici(3, t, q1, gathered.at[t], before), ici(4, t, q0, gathered.at[t], before), ici(5, right, q1, gathered.at[right], before),
        ])
        moved = [(t, both), (left, q0), (right, q1), (left, q1), (right, q0), (far, q0), (far, q1)]
        across.append([
            remote(
                gathered.at[who, rows], gathered.at[who, rows],
                sib_send.at[half, i], sib_recv.at[half, i], sibling,
            )
            for i, (who, rows) in enumerate(moved)
        ])

    def send_own(half):
        plus[half][0].start()
        minus[half][0].start()
        across[half][0].start()
        plus[half][1].start()
        minus[half][1].start()

    send_own(0)
    fetch(shard_order[2:])

    lens = lens_ref[...].astype(F32)
    earlier = iota((64, 64), 1) < iota((64, 64), 0)
    starts = jnp.sum(jnp.where(earlier, lens, 0.0), axis=1, keepdims=True)

    def lowest(block, half):
        token = (block * ROWS + half * HALF + iota((1, HALF), 1)).astype(F32)
        return token, jnp.max(jnp.where(starts <= token, starts, 0.0), axis=0, keepdims=True)

    for half in range(2):
        token, low = lowest(b, half)
        angle = freq_ref[:, 0:1] * (token - low)
        table[half, 0] = jnp.cos(angle)
        table[half, 1] = jnp.where(iota((ROT, HALF), 0) < ROT // 2, -1.0, 1.0) * jnp.sin(angle)
        for slot in range(4):
            lows[half, slot] = lowest(block_of(slot, group), half)[1]

    for copy in stat_copies:
        copy.wait_recv()
    means = stats[:, 0, :]
    whole_mean = jnp.sum(means, axis=0, keepdims=True) * 0.125
    off = means - whole_mean
    squares = jnp.sum(stats[:, 1, :], axis=0, keepdims=True) + SHARD * jnp.sum(off * off, axis=0, keepdims=True)
    inverse = lax.rsqrt(squares * (1.0 / (8 * SHARD)) + EPSILON)
    columns[0] = jnp.transpose(jnp.broadcast_to(whole_mean, (128, ROWS)))
    columns[1] = jnp.transpose(jnp.broadcast_to(inverse, (128, ROWS)))

    def compute(key, half):
        who = origin(*key)
        rows = slice(half * HALF, (half + 1) * HALF)
        product = None
        for k in range(SHARD // HALF):
            tiles = []
            for j in range(2 * k, 2 * k + 2):
                span = slice(128 * j, 128 * j + 128)
                tiles.append((
                    (gathered[who, rows, span].astype(F32) - columns[0, rows, :])
                    * columns[1, rows, :] * gain_ref[who, :, span]
                ).astype(BF16))
            depth = pl.ds(pl.multiple_of(who * SHARD + k * HALF, HALF), HALF)
            term = jnp.dot(jnp.concatenate(tiles, axis=1), wbuf[depth, :], preferred_element_type=F32)
            product = term if product is None else product + term
        if key == (0, 0):
            acc[...] = product
        else:
            acc[...] += product

    def epilogue(half):
        cosine, sine = table[half, 0], table[half, 1]
        for kind in range(3):
            turned = jnp.transpose(acc[:, kind * COLS:(kind + 1) * COLS])
            for h in range(COLS // HD):
                piece = turned[h * HD:(h + 1) * HD]
                if kind < 2:
                    top = piece[:ROT]
                    swapped = jnp.concatenate([top[ROT // 2:], top[:ROT // 2]], axis=0)
                    piece = jnp.concatenate([top * cosine + swapped * sine, piece[ROT:]], axis=0)
                qkv[half, h, kind] = piece.astype(BF16)

    pair = pl.ds(1, 2)
    kept, kv_copies, q_copies, ag_copies = [[], []], [[], []], [[], []], [[], []]

    def redistribute(half):
        copy = pltpu.make_async_copy(qkv.at[half, mine, pair], kv.at[half, group, mine], keep_sem.at[half, 0])
        copy.start()
        kept[half].append(copy)
        copy = pltpu.make_async_copy(qkv.at[half, mine, 0], qbuf.at[half, mine], keep_sem.at[half, 1])
        copy.start()
        kept[half].append(copy)
        for d in order:
            head = (mine + d) % 4
            copy = remote(
                qkv.at[half, head, pair], kv.at[half, group, mine],
                kv_send.at[half, d - 1], kv_recv.at[half, d - 1], (block_of(head, group), t),
            )
            copy.start()
            kv_copies[half].append(copy)
        for d in order:
            copy = remote(
                qkv.at[half, mine, pair], kv.at[half, group, mine],
                ag_send.at[half, 0, d - 1], ag_recv.at[half, 0, d - 1], (block_of(mine, (group + d) % 4), t),
            )
            copy.start()
            ag_copies[half].append(copy)
        for d in order:
            head = (mine + d) % 4
            copy = remote(
                qkv.at[half, head, 0], qbuf.at[half, mine],
                q_send.at[half, d - 1], q_recv.at[half, d - 1], (block_of(head, group), t),
            )
            copy.start()
            q_copies[half].append(copy)

    def relay(half, i):
        d = order[i]
        kv_copies[half][i].wait_recv()
        slot = (mine + 4 - d) % 4
        for e in order:
            copy = remote(
                kv.at[half, group, slot], kv.at[half, group, slot],
                ag_send.at[half, d, e - 1], ag_recv.at[half, d, e - 1], (block_of(mine, (group + e) % 4), t),
            )
            copy.start()
            ag_copies[half].append(copy)

    def relay_ring(half):
        plus[half][0].wait_recv()
        plus[half][2].start()
        across[half][1].start()
        minus[half][0].wait_recv()
        minus[half][2].start()
        across[half][2].start()

    def ready(key):
        for copy in loads[key]:
            copy.wait()

    for half in range(2):
        if half == 0:
            ready((0, 0))
        compute((0, 0), half)
        relay_ring(half)
        if half == 0:
            send_own(1)
            ready((0, 1))
        else:
            for copy in out_loads.values():
                copy.start()
        across[half][0].wait_recv()
        compute((0, 1), half)
        if half == 1:
            relay(0, 0)
        plus[half][1].wait_recv()
        across[half][3].start()
        minus[half][1].wait_recv()
        across[half][4].start()
        if half == 0:
            ready((3, 0))
        compute((3, 0), half)
        if half == 1:
            relay(0, 1)
        if half == 0:
            ready((1, 0))
        compute((1, 0), half)
        if half == 1:
            relay(0, 2)
        across[half][1].wait_recv()
        across[half][3].wait_recv()
        if half == 0:
            ready((3, 1))
        compute((3, 1), half)
        across[half][2].wait_recv()
        across[half][4].wait_recv()
        if half == 0:
            ready((1, 1))
        compute((1, 1), half)
        plus[half][2].wait_recv()
        across[half][5].start()
        minus[half][2].wait_recv()
        across[half][6].start()
        if half == 0:
            ready((2, 0))
        compute((2, 0), half)
        across[half][5].wait_recv()
        across[half][6].wait_recv()
        if half == 0:
            ready((2, 1))
        compute((2, 1), half)
        epilogue(half)
        redistribute(half)

    depth_index = iota((HALF, HALF), 0).astype(F32)
    query_index = iota((HALF, HALF), 1).astype(F32)

    def turn(half):
        def one(i, carry):
            keys[half, i // 4, i % 4] = jnp.transpose(kv[half, i // 4, i % 4, 0].astype(F32)).astype(BF16)
            return carry

        lax.fori_loop(0, 16, one, 0)

    def unit(slot, q_half, k_half, backs, first):
        query_block = block_of(slot, group)
        low, query = lows[q_half, slot], qbuf[q_half, slot]

        def place(back):
            key_block = query_block - back
            safe = (key_block + 16) % 16
            return key_block, (1 - c) * (safe // 4) + c * (safe % 4), (1 - c) * (safe % 4) + c * (safe // 4)

        rough = None
        for i, back in enumerate(backs):
            key_block, a, g = place(back)
            score = jnp.dot(keys[k_half, g, a], query, preferred_element_type=F32)
            allowed = depth_index >= low - (key_block * ROWS + k_half * HALF).astype(F32)
            if back == 0 and q_half == k_half:
                allowed = allowed & (depth_index <= query_index)
            score = jnp.where(allowed, score, LOWEST)
            scores[i] = score
            tallest = jnp.max(score.reshape(HALF // 8, 8, HALF), axis=0)
            rough = tallest if rough is None else jnp.maximum(rough, tallest)
        highest = jnp.max(rough, axis=0, keepdims=True)
        if not first:
            previous = peak[q_half, slot]
            highest = jnp.maximum(highest, previous)
            fade = jnp.exp2((previous - highest) * FACTOR)
        sums, mixed = None, None
        for i, back in enumerate(backs):
            _, a, g = place(back)
            weight = jnp.exp2((scores[i] - highest) * FACTOR)
            added = jnp.sum(weight.reshape(HALF // 8, 8, HALF), axis=0)
            term = jnp.dot(kv[k_half, g, a, 1], weight.astype(BF16), preferred_element_type=F32)
            sums = added if sums is None else sums + added
            mixed = term if mixed is None else mixed + term
        added = jnp.sum(sums, axis=0, keepdims=True)
        if first:
            total[q_half, slot] = added
            mix[q_half, slot] = mixed
        else:
            total[q_half, slot] = total[q_half, slot] * fade + added
            mix[q_half, slot] = mix[q_half, slot] * fade + mixed
        peak[q_half, slot] = highest

    def sweep(q_half, k_half, low_slot=0, high_slot=4):
        newest = 0 if k_half <= q_half else 1
        oldest = 9 if k_half >= q_half else 8
        backs = list(range(newest, oldest))

        def one(i, carry):
            slot = (mine + 1 + i) % 4
            unit(slot, q_half, k_half, backs, k_half == 0)
            return carry

        lax.fori_loop(low_slot, high_slot, one, 0)

    o_copies = [[], []]

    def finish(half, slot):
        return (mix[half, slot] / total[half, slot]).astype(BF16)

    def give_back(half):
        def one(i, carry):
            slot = (mine + 1 + i) % 4
            done[half, slot] = finish(half, slot)
            return carry

        lax.fori_loop(0, 3, one, 0)
        for d in order:
            slot = (mine + d) % 4
            copy = remote(
                done.at[half, slot], heads.at[half, mine],
                o_send.at[half, d - 1], o_recv.at[half, d - 1], (block_of(slot, group), t),
            )
            copy.start()
            o_copies[half].append(copy)

    def keep(half):
        heads[half, mine] = finish(half, mine)

    for copy in kept[0]:
        copy.wait()
    for copy in q_copies[0] + ag_copies[0]:
        copy.wait_recv()
    turn(0)
    sweep(0, 0, 0, 2)
    relay(1, 0)
    relay(1, 1)
    relay(1, 2)
    sweep(0, 0, 2, 4)
    for copy in kept[1]:
        copy.wait()
    for copy in q_copies[1]:
        copy.wait_recv()
    sweep(1, 0)

    page_col = jnp.sum(
        jnp.where(iota((32, 32), 0) == iota((32, 32), 1), pages_ref[...].astype(F32), 0.0), axis=1, keepdims=True
    )
    spread_pages = jnp.where(iota((32, ROWS), 0) == iota((32, ROWS), 1) // PAGE, page_col, 0.0)
    shift = (iota((1, ROWS), 1) % PAGE - b * ROWS).astype(F32)
    target = jnp.sum(spread_pages, axis=0, keepdims=True) * PAGE + shift
    chosen = (iota((ROWS, ROWS), 0).astype(F32) == target).astype(F32).astype(BF16)
    for kind in range(2):
        moved = None
        for half in range(2):
            source = jnp.concatenate([qkv[half, h, kind + 1] for h in range(4)], axis=0)
            term = lax.dot_general(
                chosen[:, half * HALF:(half + 1) * HALF], source, (((1,), (1,)), ((), ())),
                preferred_element_type=F32,
            )
            moved = term if moved is None else moved + term
        page_ref[kind] = moved.astype(BF16).reshape(ROWS // PAGE, PAGE, COLS)

    def turn_one(g, a):
        keys[1, g, a] = jnp.transpose(kv[1, g, a, 0].astype(F32)).astype(BF16)

    for a in range(4):
        turn_one(group, a)
    for n, copy in enumerate(ag_copies[1]):
        copy.wait_recv()
        d = order[n // 3 - 1] if n >= 3 else 0
        turn_one((group + 4 - order[n % 3]) % 4, (mine + 4 - d) % 4)
    sweep(0, 1, 0, 3)
    give_back(0)
    sweep(0, 1, 3, 4)
    keep(0)

    rs_order = (2, 1, 3, 0)
    ring, across_sums = [{}, {}], [[], []]

    def product(half, key):
        return jnp.dot(x[half], wo[origin(*key)], preferred_element_type=F32)

    def tx(half, i, k):
        return gathered.at[4 + i, part(half, k)]

    def leave(half, i, k, where):
        rows = pl.ds(k * QUARTER, QUARTER)
        n = 2 * i + k
        copy = remote(tx(half, i, k), rx.at[half, i, rows], ring_send.at[half, n], ring_recv.at[half, n], where)
        copy.start()
        ring[half][(i, k)] = copy

    def first_part(half):
        for copy in o_copies[half]:
            copy.wait_recv()
        flat = jnp.concatenate([heads[half, h] for h in range(4)], axis=0).astype(F32)
        x[half] = jnp.transpose(flat).astype(BF16)

        def give(i):
            if half == 0:
                out_loads[(rs_order[i], 1)].wait()
            gathered[i, pl.ds(half * HALF, HALF), :] = product(half, (rs_order[i], 1)).astype(BF16)
            copy = remote(gathered.at[i, pl.ds(half * HALF, HALF)], sib_in.at[half, i], give_send.at[half, i], give_recv.at[half, i], sibling)
            copy.start()
            across_sums[half].append(copy)

        def own(i):
            if half == 0:
                out_loads[(rs_order[i], 0)].wait()
            value = product(half, (rs_order[i], 0))
            across_sums[half][i].wait_recv()
            return value + sib_in[half, i].astype(F32)

        give(0)
        give(1)
        gathered[4, pl.ds(half * HALF, HALF), :] = own(0).astype(BF16)
        leave(half, 0, 0, after)
        leave(half, 0, 1, before)
        give(2)
        value = own(1)
        tx(half, 1, 1)[...] = value[QUARTER:].astype(BF16)
        leave(half, 1, 1, after)
        hold[half, 0] = value[:QUARTER]
        give(3)
        value = own(2)
        tx(half, 2, 0)[...] = value[:QUARTER].astype(BF16)
        leave(half, 2, 0, before)
        hold[half, 1] = value[QUARTER:]
        far_hold[half] = own(3)

    def second_part(half):
        ring[half][(0, 0)].wait_recv()
        tx(half, 1, 0)[...] = (hold[half, 0] + rx[half, 0, :QUARTER].astype(F32)).astype(BF16)
        leave(half, 1, 0, after)
        ring[half][(0, 1)].wait_recv()
        tx(half, 2, 1)[...] = (hold[half, 1] + rx[half, 0, QUARTER:].astype(F32)).astype(BF16)
        leave(half, 2, 1, before)

    def last_part(half):
        for key in ((1, 1), (2, 0), (1, 0), (2, 1)):
            ring[half][key].wait_recv()
        out_ref[half * HALF:(half + 1) * HALF, :] = (
            far_hold[half] + rx[half, 1].astype(F32) + rx[half, 2].astype(F32)
        ).astype(BF16)

    sweep(1, 1, 0, 2)
    for half in range(2):
        for copy in plus[half] + minus[half] + across[half]:
            copy.wait_send()
    first_part(0)
    sweep(1, 1, 2, 3)
    give_back(1)
    second_part(0)
    sweep(1, 1, 3, 4)
    keep(1)
    first_part(1)
    last_part(0)
    second_part(1)
    last_part(1)

    for copy in stat_copies:
        copy.wait_send()
    for half in range(2):
        for copy in kv_copies[half] + q_copies[half] + ag_copies[half] + o_copies[half]:
            copy.wait_send()
        for copy in across_sums[half] + list(ring[half].values()):
            copy.wait_send()


VMEM = pl.BlockSpec(memory_space=pltpu.VMEM)
HBM = pl.BlockSpec(memory_space=pltpu.MemorySpace.HBM)
DMA = pltpu.SemaphoreType.DMA


def per_device(hidden_in, ln_gain, w_qkv, w_out, doc_lengths, segment_ids, pair_table, page_table):
    frequency = 10000.0 ** (-(2.0 * (np.arange(ROT) % (ROT // 2))) / ROT)
    frequency = jnp.asarray(np.repeat(frequency[:, None], 128, axis=1), F32)
    scratch = [
        pltpu.VMEM((8, 1, SHARD), F32),
        pltpu.VMEM((1, 64), jnp.int32),
        pltpu.VMEM((1, 32), jnp.int32),
        pltpu.VMEM((ROT, 128), F32),
        pltpu.VMEM((8, ROWS, SHARD), BF16),
        pltpu.VMEM((8 * SHARD, 3 * COLS), BF16),
        pltpu.VMEM((HALF, 3 * COLS), F32),
        pltpu.VMEM((8, 8, ROWS), F32),
        pltpu.VMEM((2, ROWS, 128), F32),
        pltpu.VMEM((2, 2, ROT, HALF), F32),
        pltpu.VMEM((2, 4, 3, HD, HALF), BF16),
        pltpu.VMEM((2, 4, HD, HALF), BF16),
        pltpu.VMEM((2, 4, 4, 2, HD, HALF), BF16),
        pltpu.VMEM((2, 4, 4, HALF, HD), BF16),
        pltpu.VMEM((2, 4, 1, HALF), F32),
        pltpu.VMEM((9, HALF, HALF), F32),
        pltpu.VMEM((2, 4, 1, HALF), F32),
        pltpu.VMEM((2, 4, 1, HALF), F32),
        pltpu.VMEM((2, 4, HD, HALF), F32),
        pltpu.VMEM((2, 4, HD, HALF), BF16),
        pltpu.VMEM((2, 4, HD, HALF), BF16),
        pltpu.VMEM((8, COLS, SHARD), BF16),
        pltpu.VMEM((2, HALF, COLS), BF16),
        pltpu.VMEM((2, 4, HALF, SHARD), BF16),
        pltpu.VMEM((2, 3, HALF, SHARD), BF16),
        pltpu.VMEM((2, 2, QUARTER, SHARD), F32),
        pltpu.VMEM((2, HALF, SHARD), F32),
        DMA((8, 3)), DMA((8,)), DMA, DMA((4,)), DMA((7,)), DMA((7,)), DMA((2, 6)), DMA((2, 6)), DMA((2, 7)), DMA((2, 7)),
        DMA((2, 2)), DMA((2, 3)), DMA((2, 3)), DMA((2, 3)), DMA((2, 3)), DMA((2, 4, 3)), DMA((2, 4, 3)),
        DMA((2, 3)), DMA((2, 3)), DMA((2, 4)), DMA((2, 4)), DMA((2, 6)), DMA((2, 6)),
    ]
    attn_out, pages = pl.pallas_call(
        layer_kernel,
        out_shape=(
            jax.ShapeDtypeStruct((ROWS, SHARD), BF16),
            jax.ShapeDtypeStruct((2, ROWS // PAGE, PAGE, COLS), BF16),
        ),
        in_specs=[HBM] * 7,
        out_specs=(VMEM, VMEM),
        scratch_shapes=scratch,
        compiler_params=pltpu.CompilerParams(
            collective_id=0, has_side_effects=True, vmem_limit_bytes=49 * 1024 * 1024
        ),
        name="layer",
    )(*[
        pltpu.with_memory_space_constraint(operand, pltpu.MemorySpace.HBM)
        for operand in (
            hidden_in, ln_gain.reshape(8, 1, SHARD), doc_lengths.reshape(1, 64), page_table.reshape(1, 32), frequency,
            jnp.transpose(w_qkv, (1, 0, 2)), w_out,
        )
    ])
    return attn_out, pages


def solution(mesh):
    placed = (P("blk", "tp"), P(), P(None, None, "tp"), P("tp", None), P(), P("blk"), P(), P("blk"))
    return jax.shard_map(
        per_device,
        mesh=mesh,
        in_specs=placed,
        out_specs=(P("blk", "tp"), P(None, "blk", None, "tp")),
        check_vma=False,
    )
```
